32 devices in a mesh: tm: 8 (over z, x), head: 4 (over y, core).
Axes of the slice: x: 2, y: 2, z: 4, core: 2. Of those that a mesh axis runs over, the one named last changes fastest.
Arguments:
- tokens_in: bfloat16 [4096, 1024], P('tm', 'head'), may hold values from -12 to 12
- conv_weight: bfloat16 [16, 192, 64], P('head'), may hold values from -0.4375 to 0.4375
- conv_bias: float32 [1024], P('head'), may hold values from -3 to 3
- norm_gain: bfloat16 [1024], P('head'), may hold values from 0.099609375 to 1.8984375
- w_query: bfloat16 [1024, 1024], P(None, 'head')
- w_key: bfloat16 [1024, 1024], P(None, 'head')
- w_value: bfloat16 [1024, 1024], P(None, 'head'), may hold values from -0.1875 to 0.1875
- w_out: bfloat16 [1024, 1024], P('head'), may hold values from -0.1875 to 0.1875
- valid_count: int32 [4], replicated, may hold values from 512 to 1024, as said below
Outputs:
- block_out: bfloat16 [4096, 1024], P('tm', 'head')
The draws below stay inside these ranges and needn't reach their ends.
Inputs may be any that keep to these rules, and one draw needn't show every extreme that they name: `valid_count`: in every draw some stretch is fully valid and some stretch has exactly 512 valid tokens.
All inputs are finite; a program needn't handle non-finite values.
Results may differ from the reference program's by a relative error of at most 0.019.
Values may be sent and summed in bfloat16 or wider, within the bound.
No kernel may reach another device: no remote copies, remote signals or barrier semaphores. Data moves between devices by JAX's collectives and lax.ppermute only.
A program may use at most 192 MiB of HBM per device.

```python
import jax
import jax.numpy as jnp
from jax import lax

D = 1024
HEADS = 16
HEAD_DIM = 64
GROUPS = 16
KERNEL = 3
DILATION = 4
STRETCH = 1024
WINDOW = 8
GROUP_WIDTH = 64
TOKENS = 4096
NCHUNK = 4


def make_pair(key):
    base = jax.random.normal(jax.random.fold_in(key, 11), (D, D), jnp.float32) / D ** 0.5
    other = jax.random.normal(jax.random.fold_in(key, 12), (D, D), jnp.float32) / D ** 0.5
    return (other, base)


def draw_w_query(key, part):
    return make_pair(key)[0].astype(jnp.bfloat16)


def draw_w_key(key, part):
    return make_pair(key)[1].astype(jnp.bfloat16)


def draw_tokens_in(key, part):
    frac = jnp.arange(D, dtype=jnp.float32) / (D - 1)
    feature_scale = 0.5 * jnp.exp(frac * jnp.log(4.0))
    noise = jax.random.truncated_normal(jax.random.fold_in(key, 32), -6.0, 6.0, (TOKENS, D), jnp.float32)
    return (noise * feature_scale[None, :]).astype(jnp.bfloat16)


def draw_valid_count(key, part):
    drawn = jax.random.randint(jax.random.fold_in(key, 21), (NCHUNK,), STRETCH // 2, STRETCH + 1, dtype=jnp.int32)
    order = jax.random.permutation(jax.random.fold_in(key, 22), NCHUNK).astype(jnp.int32)
    drawn = drawn.at[order[0]].set(STRETCH)
    drawn = drawn.at[order[1]].set(STRETCH // 2)
    return drawn.astype(jnp.int32)


def steps_of(own_key, dims, split, least, top_value):
    def one(position, blocks):
        heights = jax.random.uniform(jax.random.fold_in(jax.random.fold_in(own_key, 6), position), (blocks,), jnp.float32, least / len(split), top_value / len(split))
        return jnp.repeat(jnp.exp(heights), dims[position] // blocks).reshape((-1,) + (1,) * (len(dims) - position - 1))

    gain = one(*split[0])
    for cut in split[1:]:
        gain = gain * one(*cut)
    return gain


def normal_values(key, shape, width, bound, shards=(), kind=jnp.bfloat16):
    values = jax.random.normal(key, shape, jnp.float32) * width
    if len(shards) > 0:
        values = steps_of(key, shape, shards, -0.22, 0.18) * values
    return jnp.clip(values, min=-bound, max=bound).astype(kind)


def setup_inputs(seed: int = 0) -> dict:
    keys = jax.random.split(jax.random.key(seed), 10)
    return {
        "tokens_in": draw_tokens_in(jax.random.fold_in(keys[9], 71), 0),
        "conv_weight": normal_values(keys[1], (GROUPS, KERNEL * GROUP_WIDTH, GROUP_WIDTH), (KERNEL * GROUP_WIDTH) ** -0.5, 0.4375, ((0, 4),)),
        "conv_bias": normal_values(keys[2], (D,), 0.5, 3.0, ((0, 4),), jnp.float32),
        "norm_gain": jnp.clip(1.0 + 0.18 * jax.random.normal(keys[3], (D,), jnp.float32), 0.099609375, 1.8984375).astype(jnp.bfloat16),
        "w_query": draw_w_query(jax.random.fold_in(keys[9], 71), 0),
        "w_key": draw_w_key(jax.random.fold_in(keys[9], 71), 0),
        "w_value": normal_values(keys[6], (D, D), D ** -0.5, 0.1875, ((1, 4),)),
        "w_out": normal_values(keys[7], (D, D), D ** -0.5, 0.1875, ((0, 4),)),
        "valid_count": draw_valid_count(jax.random.fold_in(keys[9], 71), 0),
    }


def reference(tokens_in, conv_weight, conv_bias, norm_gain, w_query, w_key, w_value, w_out, valid_count):
    rim = (KERNEL - 1) * DILATION
    padded = jnp.pad(tokens_in, ((rim, 0), (0, 0)))
    taps = [padded[j * DILATION:j * DILATION + TOKENS] for j in range(KERNEL)]
    stacked = jnp.stack(taps, 1).reshape(TOKENS, KERNEL, GROUPS, GROUP_WIDTH)
    stacked = jnp.transpose(stacked, (0, 2, 1, 3)).reshape(TOKENS, GROUPS, KERNEL * GROUP_WIDTH)
    conv_term = jnp.einsum('tgi,gio->tgo', stacked.astype(jnp.float32), conv_weight.astype(jnp.float32)).reshape(TOKENS, D)
    mixed = (tokens_in.astype(jnp.float32) + jax.nn.gelu(conv_term + conv_bias, approximate=True)).astype(jnp.bfloat16)
    mixed32 = mixed.astype(jnp.float32)
    mean_sq = lax.optimization_barrier(jnp.mean(mixed32 * mixed32, axis=1, keepdims=True))
    normed = (mixed32 * lax.rsqrt(mean_sq + 1e-06) * norm_gain.astype(jnp.float32)).astype(jnp.bfloat16)
    query = jnp.dot(normed, w_query, preferred_element_type=jnp.float32).astype(jnp.bfloat16)
    key = jnp.dot(normed, w_key, preferred_element_type=jnp.float32).astype(jnp.bfloat16)
    value = jnp.dot(normed, w_value, preferred_element_type=jnp.float32).astype(jnp.bfloat16)
    front = WINDOW * STRETCH
    span = (WINDOW + 1) * STRETCH
    key_pad = jnp.pad(key, ((front, 0), (0, 0)))
    value_pad = jnp.pad(value, ((front, 0), (0, 0)))
    scale = 1.0 / HEAD_DIM ** 0.5

    def one(index):
        stretch = index // HEADS
        head_id = index % HEADS
        row0 = (stretch * STRETCH).astype(jnp.int32)
        col0 = (head_id * HEAD_DIM).astype(jnp.int32)
        q_blk = lax.dynamic_slice(query, (row0, col0), (STRETCH, HEAD_DIM))
        k_blk = lax.dynamic_slice(key_pad, (row0, col0), (span, HEAD_DIM))
        v_blk = lax.dynamic_slice(value_pad, (row0, col0), (span, HEAD_DIM))
        scores = jnp.dot(q_blk, k_blk.T, preferred_element_type=jnp.float32) * scale
        q_pos = row0 + jnp.arange(STRETCH, dtype=jnp.int32)
        k_pos = row0 - front + jnp.arange(span, dtype=jnp.int32)
        k_stretch = jnp.clip(k_pos // STRETCH, 0, NCHUNK - 1).astype(jnp.int32)
        counts = jnp.where(k_pos >= 0, valid_count[k_stretch], 0)
        key_ok = (k_pos >= 0) & (k_pos % STRETCH < counts)
        allowed = key_ok[None, :] & (k_pos[None, :] <= q_pos[:, None])
        top = lax.optimization_barrier(jnp.max(jnp.where(allowed, scores, -1e+30), axis=1, keepdims=True))
        weights = jnp.where(allowed, jnp.exp(scores - top), 0.0)
        total = lax.optimization_barrier(jnp.sum(weights, axis=1, keepdims=True))
        out = jnp.dot(weights.astype(jnp.bfloat16), v_blk, preferred_element_type=jnp.float32) / total
        return out.astype(jnp.bfloat16)
    blocks = lax.map(one, jnp.arange(NCHUNK * HEADS, dtype=jnp.int32))
    blocks = blocks.reshape(NCHUNK, HEADS, STRETCH, HEAD_DIM)
    attended = jnp.transpose(blocks, (0, 2, 1, 3)).reshape(TOKENS, D)
    proj = jnp.dot(attended, w_out, preferred_element_type=jnp.float32)
    return (mixed32 + proj).astype(jnp.bfloat16)
```

```python
import functools

import jax
import jax.numpy as jnp
from jax import lax
from jax.experimental import pallas as pl
from jax.experimental.pallas import tpu as pltpu
from jax.sharding import PartitionSpec as P

D = 1024
HEAD_DIM = 64
KERNEL = 3
DILATION = 4
STRETCH = 1024
WINDOW = 8
RIM = (KERNEL - 1) * DILATION
GAIN_ROWS = 8
NEG = -1e30
F32 = jnp.float32
BF16 = jnp.bfloat16


def from_behind(value, axis, steps):
    count = lax.axis_size(axis)
    first, last = (max(0, -steps), min(count, count - steps))
    return lax.ppermute(value, axis, [(source, source + steps) for source in range(first, last)])


def ring_on_device(
    tokens_in, conv_weight, conv_bias, norm_gain, w_query, w_key, w_value, w_out, valid_count
):
    tok = tokens_in.shape[0]
    local_groups = conv_weight.shape[0]
    width = conv_weight.shape[2]
    rim = (KERNEL - 1) * DILATION
    before = from_behind(tokens_in[tok - rim :], "tm", 1)
    extended = jnp.concatenate([before, tokens_in], axis=0)
    taps = [extended[j * DILATION : j * DILATION + tok] for j in range(KERNEL)]
    stacked = jnp.stack(taps, 1).reshape(tok, KERNEL, local_groups, width)
    stacked = jnp.transpose(stacked, (0, 2, 1, 3)).reshape(tok, local_groups, KERNEL * width)
    conv_term = jnp.einsum("tgi,gio->tgo", stacked, conv_weight, preferred_element_type=jnp.float32)
    conv_term = conv_term.reshape(tok, local_groups * width)
    mixed = (
        tokens_in.astype(jnp.float32) + jax.nn.gelu(conv_term + conv_bias, approximate=True)
    ).astype(jnp.bfloat16)
    mixed32 = mixed.astype(jnp.float32)
    weights_all = jnp.concatenate([w_query, w_key, w_value], axis=1)
    local_cols = w_query.shape[1]
    square_part = jnp.sum(mixed32 * mixed32, axis=1)
    square_tot = lax.psum(square_part, "head")
    rstd = lax.rsqrt(square_tot / D + 1e-06)
    normed = (mixed32 * rstd[:, None] * norm_gain.astype(jnp.float32)).astype(jnp.bfloat16)
    projected = jnp.dot(
        lax.all_gather(normed, "head", axis=1, tiled=True),
        weights_all,
        preferred_element_type=jnp.float32,
    )
    projected = projected.astype(jnp.bfloat16)
    local_heads = local_cols // HEAD_DIM
    query = projected[:, :local_cols].reshape(tok, local_heads, HEAD_DIM)
    keys_own = projected[:, local_cols : 2 * local_cols]
    values_own = projected[:, 2 * local_cols :]
    scale = 1.0 / HEAD_DIM**0.5
    shard = lax.axis_index("tm")
    q_pos = shard * tok + jnp.arange(tok, dtype=jnp.int32)
    stretch_ids = jnp.arange(valid_count.shape[0], dtype=jnp.int32)

    def attend(state, keys_blk, values_blk, source):
        top, total, accum = state
        k_pos = source * tok + jnp.arange(tok, dtype=jnp.int32)
        k_stretch = jnp.where(k_pos >= 0, k_pos // STRETCH, -1)
        counts = jnp.sum(
            jnp.where(k_stretch[:, None] == stretch_ids[None, :], valid_count[None, :], 0), axis=1
        )
        key_ok = (k_pos >= 0) & (k_pos % STRETCH < counts)
        allowed = key_ok[None, :] & (k_pos[None, :] <= q_pos[:, None])
        allowed = allowed & (k_pos[None, :] // STRETCH >= q_pos[:, None] // STRETCH - WINDOW)
        keys3 = keys_blk.reshape(tok, local_heads, HEAD_DIM)
        values3 = values_blk.reshape(tok, local_heads, HEAD_DIM)
        scores = (
            jnp.einsum("qhd,khd->hqk", query, keys3, preferred_element_type=jnp.float32) * scale
        )
        block_top = jnp.max(jnp.where(allowed[None], scores, -1e30), axis=2)
        new_top = jnp.maximum(top, block_top)
        weights = jnp.where(allowed[None], jnp.exp(scores - new_top[:, :, None]), 0.0)
        factor = jnp.exp(top - new_top)
        total = total * factor + jnp.sum(weights, axis=2)
        accum = accum * factor[:, :, None] + jnp.einsum(
            "hqk,khd->hqd",
            weights.astype(jnp.bfloat16),
            values3,
            preferred_element_type=jnp.float32,
        )
        return (new_top, total, accum)

    state = (
        jnp.full((local_heads, tok), -1e30, jnp.float32),
        jnp.zeros((local_heads, tok), jnp.float32),
        jnp.zeros((local_heads, tok, HEAD_DIM), jnp.float32),
    )
    state = attend(state, keys_own, values_own, shard)
    reach = (WINDOW * STRETCH + max(STRETCH - tok, 0) + tok - 1) // tok
    steps_back = min(reach, lax.axis_size("tm") - 1)

    def relay_step(step, carry):
        keys_blk, values_blk, inner = carry
        keys_blk, values_blk = from_behind((keys_blk, values_blk), "tm", 1)
        inner = attend(inner, keys_blk, values_blk, shard - step)
        return (keys_blk, values_blk, inner)

    carried = lax.fori_loop(1, steps_back + 1, relay_step, (keys_own, values_own, state))
    state = carried[2]
    top, total, accum = state
    attended = (accum / total[:, :, None]).astype(jnp.bfloat16)
    attended = jnp.transpose(attended, (1, 0, 2)).reshape(tok, local_cols)
    partial_proj = jnp.dot(attended, w_out, preferred_element_type=jnp.float32)
    proj = lax.psum_scatter(
        partial_proj.astype(jnp.bfloat16), "head", scatter_dimension=1, tiled=True
    ).astype(jnp.float32)
    return (mixed32 + proj).astype(jnp.bfloat16)


def swap(value, bit):
    return lax.ppermute(value, "head", [(i, i ^ bit) for i in range(lax.axis_size("head"))])


def dot32(a, b):
    return jnp.dot(a, b, preferred_element_type=F32)


def dot_nt(a, b):
    return lax.dot_general(a, b, (((1,), (1,)), ((), ())), preferred_element_type=F32)


def lane_iota(shape):
    return lax.broadcasted_iota(jnp.int32, shape, 1)


def conv_kernel(halo_ref, x_ref, w_ref, b_ref, o_ref):
    rows = o_ref.shape[0]
    groups, _, width = w_ref.shape
    chans = groups * width
    x32 = x_ref[0:rows, :].astype(F32)
    ext = jnp.concatenate([halo_ref[...].astype(F32), x32], axis=0)
    acc = jnp.zeros((rows, chans), F32)
    for j in range(KERNEL):
        tap = ext[j * DILATION : j * DILATION + rows].astype(BF16)
        bands = []
        for g in range(groups):
            blk = w_ref[g, j * width : (j + 1) * width, :].astype(F32)
            parts = []
            if g > 0:
                parts.append(jnp.zeros((width, g * width), F32))
            parts.append(blk)
            if g < groups - 1:
                parts.append(jnp.zeros((width, (groups - 1 - g) * width), F32))
            bands.append(jnp.concatenate(parts, axis=1))
        acc += dot32(tap, jnp.concatenate(bands, axis=0).astype(BF16))
    act = jax.nn.gelu(acc + b_ref[...], approximate=True)
    o_ref[...] = (x32 + act).astype(BF16)


def conv_mix(halo, x, weight, bias, rows):
    return pl.pallas_call(
        conv_kernel,
        out_shape=jax.ShapeDtypeStruct((rows, x.shape[1]), BF16),
        in_specs=[pl.BlockSpec(memory_space=pltpu.VMEM)] * 4,
        out_specs=pl.BlockSpec(memory_space=pltpu.VMEM),
    )(halo, x, weight, bias)


def qkv_kernel(
    pos_ref, a_ref, b_ref, y_ref, fa_ref, fb_ref, fy_ref,
    wq0, wk0, wv0, wq1, wk1, wv1, o_ref,
):
    half = o_ref.shape[1] * 2 // 3
    cols = a_ref.shape[1]
    core, ychip = pos_ref[0], pos_ref[1]
    parts = [
        (a_ref[...], fa_ref[...], 2 * ychip + core),
        (b_ref[...], fb_ref[...], 2 * ychip + 1 - core),
        (y_ref[:, :cols], fy_ref[:, :cols], 2 * (1 - ychip) + core),
        (y_ref[:, cols:], fy_ref[:, cols:], 2 * (1 - ychip) + 1 - core),
    ]
    rows = lax.broadcasted_iota(jnp.int32, (RIM, cols), 0)
    fixed = core == 0
    xs, square = [], jnp.zeros((half, cols), F32)
    for main, fix, group in parts:
        x = main[:half].astype(F32)
        top = jnp.where(jnp.logical_and(fixed, rows >= 0), fix.astype(F32), x[:RIM])
        x = jnp.concatenate([top, x[RIM:]], axis=0)
        gain = main[half : half + 1].astype(F32)
        square += x * x
        xs.append((x, gain, group))
    rstd = lax.rsqrt(jnp.sum(square, axis=1, keepdims=True) / (4 * cols) + 1e-06)
    normed = [((x * rstd * gain).astype(BF16), group) for x, gain, group in xs]

    def project(w):
        total = None
        for x, group in normed:
            term = dot32(x, w[pl.ds(pl.multiple_of(group * cols, cols), cols), :])
            total = term if total is None else total + term
        return total.astype(BF16)

    for first, (wq, wk, wv) in ((core, (wq0, wk0, wv0)), (1 - core, (wq1, wk1, wv1))):
        q, k, v = project(wq), project(wk), project(wv)
        q = (q.astype(F32) * (1.0 / HEAD_DIM**0.5)).astype(BF16)
        heads = cols // HEAD_DIM
        for j in range(heads):
            lanes = slice(j * HEAD_DIM, (j + 1) * HEAD_DIM)
            head = first * heads + j
            o_ref[head, 0:half, :] = jnp.concatenate([k[:, lanes], v[:, lanes]], axis=1)
            o_ref[head, half : half + half // 2, :] = jnp.concatenate(
                [q[: half // 2, lanes], q[half // 2 :, lanes]], axis=1
            )


def attend_kernel(pos_ref, valid_ref, own_ref, oth_ref, o_ref, kb, vb, sc):
    blocks = own_ref.shape[0]
    half = o_ref.shape[1] * 2
    core = pos_ref[0]
    lane = lane_iota((half, 128))
    row = lax.broadcasted_iota(jnp.int32, (half, 128), 0)
    for t in range(blocks):
        for side, ref in ((0, own_ref), (1, oth_ref)):
            kv = ref[t, 0:half, :].astype(F32)
            part = core if side == 0 else 1 - core
            offset = (2 * half * t) % STRETCH + part * half
            ok = row + offset < valid_ref[(2 * half * t) // STRETCH]
            bias = jnp.where(jnp.logical_and(lane == HEAD_DIM, jnp.logical_not(ok)), NEG, 0.0)
            kb[2 * t + side] = jnp.where(lane < HEAD_DIM, kv, bias).astype(BF16)
            vb[2 * t + side] = jnp.where(lane < HEAD_DIM, 1.0, kv).astype(BF16)
    qrow = lax.broadcasted_iota(jnp.int32, (half, half), 0)
    kcol = lane_iota((half, half))
    ahead = jnp.where(core == 0, NEG, 0.0)
    halfrows = half // 2
    lane_h = lane_iota((halfrows, 128))
    pad = jnp.where(lane_h == HEAD_DIM, 1.0, 0.0)
    for t in range(blocks):
        packed = own_ref[t, half:, :].astype(F32)
        q = jnp.concatenate(
            [
                jnp.where(lane_h < HEAD_DIM, packed, pad),
                jnp.where(lane_h < HEAD_DIM, pltpu.roll(packed, HEAD_DIM, 1), pad),
            ],
            axis=0,
        ).astype(BF16)
        top = jnp.full((half, 128), NEG, F32)
        for b in range(2 * t + 2):
            s = dot_nt(q, kb[b])
            if b == 2 * t:
                s = jnp.where(kcol <= qrow, s, NEG)
            if b == 2 * t + 1:
                s = s + ahead
            sc[b] = s
            for piece in range(half // 128):
                top = jnp.maximum(top, s[:, piece * 128 : (piece + 1) * 128])
        m = jnp.max(top, axis=1, keepdims=True)
        acc = jnp.zeros((half, 128), F32)
        for b in range(2 * t + 2):
            acc += dot32(jnp.exp(sc[b] - m).astype(BF16), vb[b])
        out = acc / pltpu.roll(acc, HEAD_DIM, 1)
        o_ref[t] = jnp.where(
            lane_h < HEAD_DIM, pltpu.roll(out[:halfrows], HEAD_DIM, 1), out[halfrows:]
        ).astype(BF16)


def out_kernel(pos_ref, own_ref, oth_ref, w0, w1, o_ref, *, other):
    heads = own_ref.shape[0]
    halfrows = own_ref.shape[1]
    half = 2 * halfrows
    cols = o_ref.shape[1]
    core, ychip = pos_ref[0], pos_ref[1]
    group = 2 * ((1 - ychip) if other else ychip) + core
    lanes = pl.ds(pl.multiple_of(group * cols, cols), cols)
    lane_h = lane_iota((halfrows, 128))
    for src, part in ((own_ref, core), (oth_ref, 1 - core)):
        total = None
        for first, w in ((core, w0), (1 - core, w1)):
            tops, bots = [], []
            for j in range(0, heads // 2, 2):
                a = src[first * (heads // 2) + j].astype(F32)
                b = src[first * (heads // 2) + j + 1].astype(F32)
                tops.append(jnp.where(lane_h < HEAD_DIM, a, pltpu.roll(b, HEAD_DIM, 1)))
                bots.append(jnp.where(lane_h < HEAD_DIM, pltpu.roll(a, HEAD_DIM, 1), b))
            feats = jnp.concatenate(
                [jnp.concatenate(tops, axis=1), jnp.concatenate(bots, axis=1)], axis=0
            ).astype(BF16)
            term = dot32(feats, w[:, lanes])
            total = term if total is None else total + term
        o_ref[pl.ds(pl.multiple_of(part * half, half), half), :] = total.astype(o_ref.dtype)


def vmem_specs(scalars, arrays):
    return [pl.BlockSpec(memory_space=pltpu.SMEM)] * scalars + [
        pl.BlockSpec(memory_space=pltpu.VMEM)
    ] * arrays


def on_device(
    tokens_in, conv_weight, conv_bias, norm_gain, w_query, w_key, w_value, w_out, valid_count
):
    tok, cols = tokens_in.shape
    half = tok // 2
    ranks = lax.axis_size("tm")
    head_at = lax.axis_index("head")
    core, ychip = head_at % 2, head_at // 2
    pos = jnp.stack([core, ychip]).astype(jnp.int32)
    bias = conv_bias.reshape(1, cols)

    halo = from_behind(tokens_in[tok - RIM :], "tm", 1)
    wq1, wk1, wv1, wo1 = swap((w_query, w_key, w_value, w_out), 1)
    mixed = conv_mix(jnp.zeros((RIM, cols), BF16), tokens_in, conv_weight, bias, tok)
    gain = jnp.broadcast_to(norm_gain[None, :], (GAIN_ROWS, cols))
    halves = mixed.reshape(2, half, cols)
    mine = jnp.concatenate([jnp.where(core == 0, halves[0], halves[1]), gain], axis=0)
    theirs = jnp.concatenate([jnp.where(core == 0, halves[1], halves[0]), gain], axis=0)
    beside = swap(theirs, 1)
    across = swap(jnp.concatenate([mine, beside], axis=1), 2)
    fix = conv_mix(halo, tokens_in[:RIM], conv_weight, bias, RIM)
    fix_beside = swap(fix, 1)
    fix_across = swap(jnp.concatenate([fix, fix_beside], axis=1), 2)

    packed = pl.pallas_call(
        qkv_kernel,
        out_shape=jax.ShapeDtypeStruct((ranks, half + half // 2, 2 * HEAD_DIM), BF16),
        in_specs=vmem_specs(1, 12),
        out_specs=pl.BlockSpec(memory_space=pltpu.VMEM),
        compiler_params=pltpu.CompilerParams(vmem_limit_bytes=40 << 20),
    )(
        pos, mine, beside, across, fix, fix_beside, fix_across,
        w_query, w_key, w_value, wq1, wk1, wv1,
    )
    own = lax.all_to_all(packed, "tm", 0, 0)
    oth = swap(own, 1)
    attended = pl.pallas_call(
        attend_kernel,
        out_shape=jax.ShapeDtypeStruct((ranks, half // 2, 2 * HEAD_DIM), BF16),
        in_specs=vmem_specs(2, 2),
        out_specs=pl.BlockSpec(memory_space=pltpu.VMEM),
        scratch_shapes=[
            pltpu.VMEM((2 * ranks, half, 128), BF16),
            pltpu.VMEM((2 * ranks, half, 128), BF16),
            pltpu.VMEM((2 * ranks, half, half), F32),
        ],
        compiler_params=pltpu.CompilerParams(vmem_limit_bytes=40 << 20),
    )(pos, valid_count, own, oth)
    back = lax.all_to_all(attended, "tm", 0, 0)
    back_beside = swap(back, 1)

    def project(other, dtype):
        return pl.pallas_call(
            functools.partial(out_kernel, other=other),
            out_shape=jax.ShapeDtypeStruct((tok, cols), dtype),
            in_specs=vmem_specs(1, 4),
            out_specs=pl.BlockSpec(memory_space=pltpu.VMEM),
        )(pos, back, back_beside, w_out, wo1)

    proj_across = swap(project(True, BF16), 2)
    proj = project(False, F32) + proj_across.astype(F32)
    whole = jnp.concatenate([fix, mixed[RIM:]], axis=0).astype(F32)
    return (whole + proj).astype(BF16)


def solution(mesh):
    ranks, heads = mesh.shape["tm"], mesh.shape["head"]

    def body(*args):
        tokens_in, conv_weight, *_ = args
        tok, cols = tokens_in.shape
        fits = heads == 4 and cols == 4 * HEAD_DIM and ranks == 2 * (cols // HEAD_DIM)
        fits = fits and tok == 512 and ranks * tok <= (WINDOW + 1) * STRETCH
        return on_device(*args) if fits else ring_on_device(*args)

    return jax.shard_map(
        body,
        mesh=mesh,
        in_specs=(
            P("tm", "head"),
            P("head", None, None),
            P("head"),
            P("head"),
            P(None, "head"),
            P(None, "head"),
            P(None, "head"),
            P("head", None),
            P(),
        ),
        out_specs=P("tm", "head"),
        check_vma=False,
    )
```

```python
import functools

import jax
import jax.numpy as jnp
from jax import lax
from jax.experimental import pallas as pl
from jax.experimental.pallas import tpu as pltpu
from jax.sharding import PartitionSpec as P

D = 1024
HEAD_DIM = 64
KERNEL = 3
DILATION = 4
STRETCH = 1024
WINDOW = 8
RIM = (KERNEL - 1) * DILATION
GAIN_ROWS = 8
NEG = -1e30
F32 = jnp.float32
BF16 = jnp.bfloat16


def from_behind(value, axis, steps):
    count = lax.axis_size(axis)
    first, last = (max(0, -steps), min(count, count - steps))
    return lax.ppermute(value, axis, [(source, source + steps) for source in range(first, last)])


def ring_on_device(
    tokens_in, conv_weight, conv_bias, norm_gain, w_query, w_key, w_value, w_out, valid_count
):
    tok = tokens_in.shape[0]
    local_groups = conv_weight.shape[0]
    width = conv_weight.shape[2]
    rim = (KERNEL - 1) * DILATION
    before = from_behind(tokens_in[tok - rim :], "tm", 1)
    extended = jnp.concatenate([before, tokens_in], axis=0)
    taps = [extended[j * DILATION : j * DILATION + tok] for j in range(KERNEL)]
    stacked = jnp.stack(taps, 1).reshape(tok, KERNEL, local_groups, width)
    stacked = jnp.transpose(stacked, (0, 2, 1, 3)).reshape(tok, local_groups, KERNEL * width)
    conv_term = jnp.einsum("tgi,gio->tgo", stacked, conv_weight, preferred_element_type=jnp.float32)
    conv_term = conv_term.reshape(tok, local_groups * width)
    mixed = (
        tokens_in.astype(jnp.float32) + jax.nn.gelu(conv_term + conv_bias, approximate=True)
    ).astype(jnp.bfloat16)
    mixed32 = mixed.astype(jnp.float32)
    weights_all = jnp.concatenate([w_query, w_key, w_value], axis=1)
    local_cols = w_query.shape[1]
    square_part = jnp.sum(mixed32 * mixed32, axis=1)
    square_tot = lax.psum(square_part, "head")
    rstd = lax.rsqrt(square_tot / D + 1e-06)
    normed = (mixed32 * rstd[:, None] * norm_gain.astype(jnp.float32)).astype(jnp.bfloat16)
    projected = jnp.dot(
        lax.all_gather(normed, "head", axis=1, tiled=True),
        weights_all,
        preferred_element_type=jnp.float32,
    )
    projected = projected.astype(jnp.bfloat16)
    local_heads = local_cols // HEAD_DIM
    query = projected[:, :local_cols].reshape(tok, local_heads, HEAD_DIM)
    keys_own = projected[:, local_cols : 2 * local_cols]
    values_own = projected[:, 2 * local_cols :]
    scale = 1.0 / HEAD_DIM**0.5
    shard = lax.axis_index("tm")
    q_pos = shard * tok + jnp.arange(tok, dtype=jnp.int32)
    stretch_ids = jnp.arange(valid_count.shape[0], dtype=jnp.int32)

    def attend(state, keys_blk, values_blk, source):
        top, total, accum = state
        k_pos = source * tok + jnp.arange(tok, dtype=jnp.int32)
        k_stretch = jnp.where(k_pos >= 0, k_pos // STRETCH, -1)
        counts = jnp.sum(
            jnp.where(k_stretch[:, None] == stretch_ids[None, :], valid_count[None, :], 0), axis=1
        )
        key_ok = (k_pos >= 0) & (k_pos % STRETCH < counts)
        allowed = key_ok[None, :] & (k_pos[None, :] <= q_pos[:, None])
        allowed = allowed & (k_pos[None, :] // STRETCH >= q_pos[:, None] // STRETCH - WINDOW)
        keys3 = keys_blk.reshape(tok, local_heads, HEAD_DIM)
        values3 = values_blk.reshape(tok, local_heads, HEAD_DIM)
        scores = (
            jnp.einsum("qhd,khd->hqk", query, keys3, preferred_element_type=jnp.float32) * scale
        )
        block_top = jnp.max(jnp.where(allowed[None], scores, -1e30), axis=2)
        new_top = jnp.maximum(top, block_top)
        weights = jnp.where(allowed[None], jnp.exp(scores - new_top[:, :, None]), 0.0)
        factor = jnp.exp(top - new_top)
        total = total * factor + jnp.sum(weights, axis=2)
        accum = accum * factor[:, :, None] + jnp.einsum(
            "hqk,khd->hqd",
            weights.astype(jnp.bfloat16),
            values3,
            preferred_element_type=jnp.float32,
        )
        return (new_top, total, accum)

    state = (
        jnp.full((local_heads, tok), -1e30, jnp.float32),
        jnp.zeros((local_heads, tok), jnp.float32),
        jnp.zeros((local_heads, tok, HEAD_DIM), jnp.float32),
    )
    state = attend(state, keys_own, values_own, shard)
    reach = (WINDOW * STRETCH + max(STRETCH - tok, 0) + tok - 1) // tok
    steps_back = min(reach, lax.axis_size("tm") - 1)

    def relay_step(step, carry):
        keys_blk, values_blk, inner = carry
        keys_blk, values_blk = from_behind((keys_blk, values_blk), "tm", 1)
        inner = attend(inner, keys_blk, values_blk, shard - step)
        return (keys_blk, values_blk, inner)

    carried = lax.fori_loop(1, steps_back + 1, relay_step, (keys_own, values_own, state))
    state = carried[2]
    top, total, accum = state
    attended = (accum / total[:, :, None]).astype(jnp.bfloat16)
    attended = jnp.transpose(attended, (1, 0, 2)).reshape(tok, local_cols)
    partial_proj = jnp.dot(attended, w_out, preferred_element_type=jnp.float32)
    proj = lax.psum_scatter(
        partial_proj.astype(jnp.bfloat16), "head", scatter_dimension=1, tiled=True
    ).astype(jnp.float32)
    return (mixed32 + proj).astype(jnp.bfloat16)


def swap(value, bit):
    return lax.ppermute(value, "head", [(i, i ^ bit) for i in range(lax.axis_size("head"))])


def spread(value, m, part):
    pairs = []
    for shard in range(8):
        for head_at in range(4):
            b, low, ychip, core = shard // 4, shard % 4, head_at // 2, head_at % 2
            to = (4 * core + (low ^ m)) * 4 + 2 * ychip + (part ^ b)
            pairs.append((shard * 4 + head_at, to))
    return lax.ppermute(value, ("tm", "head"), pairs)


def dot32(a, b):
    return jnp.dot(a, b, preferred_element_type=F32)


def dot_nt(a, b):
    return lax.dot_general(a, b, (((1,), (1,)), ((), ())), preferred_element_type=F32)


def lane_iota(shape):
    return lax.broadcasted_iota(jnp.int32, shape, 1)


def gelu_mix(x32, term):
    return (x32 + jax.nn.gelu(term, approximate=True)).astype(BF16)


def conv_kernel(x_ref, w_ref, b_ref, g_ref, late_ref, early_ref, band_ref, base_ref):
    rows = x_ref.shape[0]
    half = rows // 2
    groups, width, _ = w_ref.shape
    x32 = x_ref[...].astype(F32)
    ext = jnp.concatenate([jnp.zeros((RIM, x32.shape[1]), F32), x32], axis=0)
    acc = jnp.zeros(x32.shape, F32) + b_ref[...]
    for j in range(KERNEL):
        bands = []
        for g in range(groups):
            parts = [w_ref[g, :, j * width : (j + 1) * width].astype(F32)]
            if g > 0:
                parts.insert(0, jnp.zeros((width, g * width), F32))
            if g < groups - 1:
                parts.append(jnp.zeros((width, (groups - 1 - g) * width), F32))
            bands.append(jnp.concatenate(parts, axis=1))
        band = jnp.concatenate(bands, axis=0).astype(BF16)
        band_ref[j] = band
        acc += dot_nt(ext[j * DILATION : j * DILATION + rows].astype(BF16), band)
    base_ref[0:RIM] = acc[0:RIM]
    base_ref[RIM:] = x32[0:RIM]
    mix = gelu_mix(x32, acc)
    gain = jnp.broadcast_to(g_ref[...].astype(F32), (GAIN_ROWS, x32.shape[1])).astype(BF16)
    late_ref[0:half] = mix[0:half]
    late_ref[half:] = gain
    early_ref[0:half] = mix[half:]
    early_ref[half:] = gain


def fix_kernel(halo_ref, base_ref, band_ref, late_ref, o_ref):
    halo = halo_ref[...].astype(F32)
    ext = jnp.concatenate([halo, jnp.zeros_like(halo)], axis=0)
    acc = base_ref[0:RIM]
    for j in range(KERNEL - 1):
        acc += dot_nt(ext[j * DILATION : j * DILATION + RIM].astype(BF16), band_ref[j])
    o_ref[...] = late_ref[...]
    o_ref[0:RIM] = gelu_mix(base_ref[RIM:], acc)


def qkv_kernel(pos_ref, a_ref, b_ref, y_ref, z_ref, wq, wk, wv, *rest):
    outs, pack = rest[:-1], rest[-1]
    half = a_ref.shape[0] - GAIN_ROWS
    cols = a_ref.shape[1]
    heads = cols // HEAD_DIM
    core, ychip, low = pos_ref[0], pos_ref[1], pos_ref[2]
    parts = [
        (a_ref, 2 * ychip + core),
        (b_ref, 2 * ychip + 1 - core),
        (y_ref, 2 * (1 - ychip) + core),
        (z_ref, 2 * (1 - ychip) + 1 - core),
    ]
    square = jnp.zeros((half, cols), F32)
    for ref, _ in parts:
        x = ref[0:half].astype(F32)
        square += x * x
    rstd = lax.rsqrt(jnp.sum(square, axis=1, keepdims=True) / (4 * cols) + 1e-06)
    normed = []
    for ref, group in parts:
        gain = ref[half : half + 1].astype(F32)
        normed.append(((ref[0:half].astype(F32) * rstd * gain).astype(BF16), group))

    def project(w):
        total = None
        for x, group in normed:
            term = dot32(x, w[pl.ds(pl.multiple_of(group * cols, cols), cols), :])
            total = term if total is None else total + term
        return total.astype(BF16)

    q, k, v = project(wq), project(wk), project(wv)
    q = (q.astype(F32) * (1.0 / HEAD_DIM**0.5)).astype(BF16)
    for j in range(heads):
        lanes = slice(j * HEAD_DIM, (j + 1) * HEAD_DIM)
        slot = jnp.bitwise_xor(low, j)
        pack[slot, 0:half, :] = jnp.concatenate([k[:, lanes], v[:, lanes]], axis=1)
        pack[slot, half : half + half // 2, :] = jnp.concatenate(
            [q[: half // 2, lanes], q[half // 2 :, lanes]], axis=1
        )
    for m, out in enumerate(outs):
        out[...] = pack[m]


def attend_kernel(pos_ref, valid_ref, *rest):
    own_refs, oth_refs, (o_ref, kb, vb, qs, sc) = rest[:8], rest[8:16], rest[16:]
    ranks = o_ref.shape[0]
    half = o_ref.shape[1] * 2
    halfrows = half // 2
    core, low = pos_ref[0], pos_ref[2]
    lane = lane_iota((half, 128))
    row = lax.broadcasted_iota(jnp.int32, (half, 128), 0)
    lane_h = lane_iota((halfrows, 128))
    pad = jnp.where(lane_h == HEAD_DIM, 1.0, 0.0)
    for i in range(8):
        part, m = 1 - i // 4, i % 4
        for side, ref in ((core, own_refs[i]), (1 - core, oth_refs[i])):
            shard = 4 * jnp.bitwise_xor(side, part) + jnp.bitwise_xor(low, m)
            block = 2 * shard + part
            start = block * half
            stretch = start // STRETCH
            ok = row + (start - stretch * STRETCH) < valid_ref[stretch]
            bias = jnp.where(jnp.logical_and(lane == HEAD_DIM, jnp.logical_not(ok)), NEG, 0.0)
            kv = ref[0:half, :].astype(F32)
            kb[block] = jnp.where(lane < HEAD_DIM, kv, bias).astype(BF16)
            vb[block] = jnp.where(lane < HEAD_DIM, 1.0, kv).astype(BF16)
            if ref is own_refs[i]:
                packed = ref[half:, :].astype(F32)
                qs[shard, 0:halfrows] = jnp.where(lane_h < HEAD_DIM, packed, pad).astype(BF16)
                qs[shard, halfrows:] = jnp.where(
                    lane_h < HEAD_DIM, pltpu.roll(packed, HEAD_DIM, 1), pad
                ).astype(BF16)
    qrow = lax.broadcasted_iota(jnp.int32, (half, half), 0)
    kcol = lane_iota((half, half))
    for t in range(ranks):
        part = jnp.bitwise_xor(core, t // 4)
        q = qs[t]
        top = jnp.full((half, 128), NEG, F32)
        for b in range(2 * t + 2):
            s = dot_nt(q, kb[b])
            if b >= 2 * t:
                s = jnp.where(kcol + (b - 2 * t) * half <= qrow + part * half, s, NEG)
            sc[b] = s
            for piece in range(half // 128):
                top = jnp.maximum(top, s[:, piece * 128 : (piece + 1) * 128])
        m = jnp.max(top, axis=1, keepdims=True)
        acc = jnp.zeros((half, 128), F32)
        for b in range(2 * t + 2):
            acc += dot32(jnp.exp(sc[b] - m).astype(BF16), vb[b])
        out = acc / pltpu.roll(acc, HEAD_DIM, 1)
        o_ref[t] = jnp.where(
            lane_h < HEAD_DIM, pltpu.roll(out[:halfrows], HEAD_DIM, 1), out[halfrows:]
        ).astype(BF16)


def out_kernel(pos_ref, own_ref, oth_ref, w0, w1, o_ref, *, other):
    heads = own_ref.shape[0]
    halfrows = own_ref.shape[1]
    half = 2 * halfrows
    cols = o_ref.shape[1]
    core, ychip = pos_ref[0], pos_ref[1]
    mine = jnp.bitwise_xor(core, pos_ref[3])
    group = 2 * ((1 - ychip) if other else ychip) + core
    lanes = pl.ds(pl.multiple_of(group * cols, cols), cols)
    lane_h = lane_iota((halfrows, 128))
    for src, part in ((own_ref, mine), (oth_ref, 1 - mine)):
        total = None
        for first, w in ((core, w0), (1 - core, w1)):
            tops, bots = [], []
            for j in range(0, heads // 2, 2):
                a = src[first * (heads // 2) + j].astype(F32)
                b = src[first * (heads // 2) + j + 1].astype(F32)
                tops.append(jnp.where(lane_h < HEAD_DIM, a, pltpu.roll(b, HEAD_DIM, 1)))
                bots.append(jnp.where(lane_h < HEAD_DIM, pltpu.roll(a, HEAD_DIM, 1), b))
            feats = jnp.concatenate(
                [jnp.concatenate(tops, axis=1), jnp.concatenate(bots, axis=1)], axis=0
            ).astype(BF16)
            term = dot32(feats, w[:, lanes])
            total = term if total is None else total + term
        o_ref[pl.ds(pl.multiple_of(part * half, half), half), :] = total.astype(o_ref.dtype)


def final_kernel(late_ref, early_ref, proj_ref, across_ref, o_ref):
    half = o_ref.shape[0] // 2
    for i, ref in enumerate((late_ref, early_ref)):
        rows = slice(i * half, (i + 1) * half)
        proj = proj_ref[rows] + across_ref[rows].astype(F32)
        o_ref[rows] = (ref[0:half].astype(F32) + proj).astype(BF16)


def call(kernel, outs, scalars, args, *, us, vmem=16, scratch=()):
    spaces = [pltpu.SMEM] * scalars + [pltpu.VMEM] * (len(args) - scalars)
    outs = [jax.ShapeDtypeStruct(*out) for out in outs]
    result = pl.pallas_call(
        kernel,
        out_shape=outs,
        in_specs=[pl.BlockSpec(memory_space=space) for space in spaces],
        out_specs=[pl.BlockSpec(memory_space=pltpu.VMEM)] * len(outs),
        scratch_shapes=scratch,
        compiler_params=pltpu.CompilerParams(vmem_limit_bytes=vmem << 20),
        cost_estimate=pl.CostEstimate(
            flops=int(us * 1e9), bytes_accessed=int(us * 3.6e6), transcendentals=0
        ),
    )(*args)
    return result if len(outs) > 1 else result[0]


def on_device(
    tokens_in, conv_weight, conv_bias, norm_gain, w_query, w_key, w_value, w_out, valid_count
):
    tok, cols = tokens_in.shape
    half = tok // 2
    ranks = lax.axis_size("tm")
    head_at, shard = lax.axis_index("head"), lax.axis_index("tm")
    pos = jnp.stack([head_at % 2, head_at // 2, shard % 4, shard // 4]).astype(jnp.int32)

    halo = from_behind(tokens_in[tok - RIM :], "tm", 1)
    late, early, band, base = call(
        conv_kernel,
        [
            ((half + GAIN_ROWS, cols), BF16),
            ((half + GAIN_ROWS, cols), BF16),
            ((KERNEL, cols, cols), BF16),
            ((2 * RIM, cols), F32),
        ],
        0,
        (
            tokens_in, jnp.swapaxes(conv_weight, 1, 2),
            conv_bias.reshape(1, cols), norm_gain.reshape(1, cols),
        ),
        us=2.0,
    )

    def project_half(x):
        beside, across = swap(x, 1), swap(x, 2)
        corner = swap(across, 1)
        return call(
            qkv_kernel,
            [((half + half // 2, 2 * HEAD_DIM), BF16)] * 4,
            1,
            (pos, x, beside, across, corner, w_query, w_key, w_value),
            us=1.0,
            scratch=[pltpu.VMEM((4, half + half // 2, 2 * HEAD_DIM), BF16)],
        )

    sends = list(project_half(early))
    late = call(
        fix_kernel, [((half + GAIN_ROWS, cols), BF16)], 0, (halo, base, band, late), us=0.5
    )
    sends += list(project_half(late))
    own = [spread(value, i % 4, 1 - i // 4) for i, value in enumerate(sends)]
    oth = [swap(value, 1) for value in own]
    wo1 = swap(lax.optimization_barrier((w_out, sends[0]))[0], 1)
    attended = call(
        attend_kernel,
        [((ranks, half // 2, 2 * HEAD_DIM), BF16)],
        2,
        (pos, valid_count, *own, *oth),
        us=8.0,
        vmem=24,
        scratch=[
            pltpu.VMEM((2 * ranks, half, 128), BF16),
            pltpu.VMEM((2 * ranks, half, 128), BF16),
            pltpu.VMEM((ranks, half, 128), BF16),
            pltpu.VMEM((2 * ranks, half, half), F32),
        ],
    )
    back = lax.all_to_all(attended, "tm", 0, 0)
    back_beside = swap(back, 1)

    def project(other, dtype):
        kernel = functools.partial(out_kernel, other=other)
        args = (pos, back, back_beside, w_out, wo1)
        return call(kernel, [((tok, cols), dtype)], 1, args, us=1.0)

    proj_across = swap(project(True, BF16), 2)
    return call(
        final_kernel,
        [((tok, cols), BF16)],
        0,
        (late, early, project(False, F32), proj_across),
        us=0.5,
    )


def solution(mesh):
    ranks, heads = mesh.shape["tm"], mesh.shape["head"]

    def body(*args):
        tokens_in, conv_weight, *_ = args
        tok, cols = tokens_in.shape
        fits = heads == 4 and cols == 4 * HEAD_DIM and ranks == 2 * (cols // HEAD_DIM)
        fits = fits and tok == 512 and ranks * tok <= (WINDOW + 1) * STRETCH
        return on_device(*args) if fits else ring_on_device(*args)

    return jax.shard_map(
        body,
        mesh=mesh,
        in_specs=(
            P("tm", "head"),
            P("head", None, None),
            P("head"),
            P("head"),
            P(None, "head"),
            P(None, "head"),
            P(None, "head"),
            P("head", None),
            P(),
        ),
        out_specs=P("tm", "head"),
        check_vma=False,
    )
```

```python
import functools

import jax
import jax.numpy as jnp
from jax import lax
from jax.experimental import pallas as pl
from jax.experimental.pallas import tpu as pltpu
from jax.sharding import PartitionSpec as P

D = 1024
HEAD_DIM = 64
KERNEL = 3
DILATION = 4
STRETCH = 1024
WINDOW = 8
RIM = (KERNEL - 1) * DILATION
GAIN_ROWS = 8
CONV_VMEM = 60
FIX_US = 2.0
NEG = -1e30
F32 = jnp.float32
BF16 = jnp.bfloat16


def from_behind(value, axis, steps):
    count = lax.axis_size(axis)
    first, last = (max(0, -steps), min(count, count - steps))
    return lax.ppermute(value, axis, [(source, source + steps) for source in range(first, last)])


def ring_on_device(
    tokens_in, conv_weight, conv_bias, norm_gain, w_query, w_key, w_value, w_out, valid_count
):
    tok = tokens_in.shape[0]
    local_groups = conv_weight.shape[0]
    width = conv_weight.shape[2]
    rim = (KERNEL - 1) * DILATION
    before = from_behind(tokens_in[tok - rim :], "tm", 1)
    extended = jnp.concatenate([before, tokens_in], axis=0)
    taps = [extended[j * DILATION : j * DILATION + tok] for j in range(KERNEL)]
    stacked = jnp.stack(taps, 1).reshape(tok, KERNEL, local_groups, width)
    stacked = jnp.transpose(stacked, (0, 2, 1, 3)).reshape(tok, local_groups, KERNEL * width)
    conv_term = jnp.einsum("tgi,gio->tgo", stacked, conv_weight, preferred_element_type=jnp.float32)
    conv_term = conv_term.reshape(tok, local_groups * width)
    mixed = (
        tokens_in.astype(jnp.float32) + jax.nn.gelu(conv_term + conv_bias, approximate=True)
    ).astype(jnp.bfloat16)
    mixed32 = mixed.astype(jnp.float32)
    weights_all = jnp.concatenate([w_query, w_key, w_value], axis=1)
    local_cols = w_query.shape[1]
    square_part = jnp.sum(mixed32 * mixed32, axis=1)
    square_tot = lax.psum(square_part, "head")
    rstd = lax.rsqrt(square_tot / D + 1e-06)
    normed = (mixed32 * rstd[:, None] * norm_gain.astype(jnp.float32)).astype(jnp.bfloat16)
    projected = jnp.dot(
        lax.all_gather(normed, "head", axis=1, tiled=True),
        weights_all,
        preferred_element_type=jnp.float32,
    )
    projected = projected.astype(jnp.bfloat16)
    local_heads = local_cols // HEAD_DIM
    query = projected[:, :local_cols].reshape(tok, local_heads, HEAD_DIM)
    keys_own = projected[:, local_cols : 2 * local_cols]
    values_own = projected[:, 2 * local_cols :]
    scale = 1.0 / HEAD_DIM**0.5
    shard = lax.axis_index("tm")
    q_pos = shard * tok + jnp.arange(tok, dtype=jnp.int32)
    stretch_ids = jnp.arange(valid_count.shape[0], dtype=jnp.int32)

    def attend(state, keys_blk, values_blk, source):
        top, total, accum = state
        k_pos = source * tok + jnp.arange(tok, dtype=jnp.int32)
        k_stretch = jnp.where(k_pos >= 0, k_pos // STRETCH, -1)
        counts = jnp.sum(
            jnp.where(k_stretch[:, None] == stretch_ids[None, :], valid_count[None, :], 0), axis=1
        )
        key_ok = (k_pos >= 0) & (k_pos % STRETCH < counts)
        allowed = key_ok[None, :] & (k_pos[None, :] <= q_pos[:, None])
        allowed = allowed & (k_pos[None, :] // STRETCH >= q_pos[:, None] // STRETCH - WINDOW)
        keys3 = keys_blk.reshape(tok, local_heads, HEAD_DIM)
        values3 = values_blk.reshape(tok, local_heads, HEAD_DIM)
        scores = (
            jnp.einsum("qhd,khd->hqk", query, keys3, preferred_element_type=jnp.float32) * scale
        )
        block_top = jnp.max(jnp.where(allowed[None], scores, -1e30), axis=2)
        new_top = jnp.maximum(top, block_top)
        weights = jnp.where(allowed[None], jnp.exp(scores - new_top[:, :, None]), 0.0)
        factor = jnp.exp(top - new_top)
        total = total * factor + jnp.sum(weights, axis=2)
        accum = accum * factor[:, :, None] + jnp.einsum(
            "hqk,khd->hqd",
            weights.astype(jnp.bfloat16),
            values3,
            preferred_element_type=jnp.float32,
        )
        return (new_top, total, accum)

    state = (
        jnp.full((local_heads, tok), -1e30, jnp.float32),
        jnp.zeros((local_heads, tok), jnp.float32),
        jnp.zeros((local_heads, tok, HEAD_DIM), jnp.float32),
    )
    state = attend(state, keys_own, values_own, shard)
    reach = (WINDOW * STRETCH + max(STRETCH - tok, 0) + tok - 1) // tok
    steps_back = min(reach, lax.axis_size("tm") - 1)

    def relay_step(step, carry):
        keys_blk, values_blk, inner = carry
        keys_blk, values_blk = from_behind((keys_blk, values_blk), "tm", 1)
        inner = attend(inner, keys_blk, values_blk, shard - step)
        return (keys_blk, values_blk, inner)

    carried = lax.fori_loop(1, steps_back + 1, relay_step, (keys_own, values_own, state))
    state = carried[2]
    top, total, accum = state
    attended = (accum / total[:, :, None]).astype(jnp.bfloat16)
    attended = jnp.transpose(attended, (1, 0, 2)).reshape(tok, local_cols)
    partial_proj = jnp.dot(attended, w_out, preferred_element_type=jnp.float32)
    proj = lax.psum_scatter(
        partial_proj.astype(jnp.bfloat16), "head", scatter_dimension=1, tiled=True
    ).astype(jnp.float32)
    return (mixed32 + proj).astype(jnp.bfloat16)


def swap(value, bit):
    return lax.ppermute(value, "head", [(i, i ^ bit) for i in range(lax.axis_size("head"))])


def spread(value, m, part):
    pairs = []
    for shard in range(8):
        for head_at in range(4):
            b, low, ychip, core = shard // 4, shard % 4, head_at // 2, head_at % 2
            to = (4 * core + (low ^ m)) * 4 + 2 * ychip + (part ^ b)
            pairs.append((shard * 4 + head_at, to))
    return lax.ppermute(value, ("tm", "head"), pairs)


def dot32(a, b):
    return jnp.dot(a, b, preferred_element_type=F32)


def dot_nt(a, b):
    return lax.dot_general(a, b, (((1,), (1,)), ((), ())), preferred_element_type=F32)


def lane_iota(shape):
    return lax.broadcasted_iota(jnp.int32, shape, 1)


def gelu_mix(x32, term):
    return (x32 + jax.nn.gelu(term, approximate=True)).astype(BF16)


def conv_kernel(
    x_hbm, w_hbm, b_hbm, g_hbm, late_ref, early_ref, band_ref, base_ref, edge_ref,
    x_ref, w_ref, b_ref, g_ref, sems,
):
    pairs = ((x_hbm, x_ref), (w_hbm, w_ref), (b_hbm, b_ref), (g_hbm, g_ref))
    copies = [pltpu.make_async_copy(src, dst, sems.at[i]) for i, (src, dst) in enumerate(pairs)]
    for copy in copies:
        copy.start()
    for copy in copies:
        copy.wait()
    rows = x_ref.shape[0]
    edge_ref[...] = x_ref[rows - RIM :]
    groups, width, _ = w_ref.shape
    x32 = x_ref[...].astype(F32)
    ext = jnp.concatenate([jnp.zeros((RIM, x32.shape[1]), F32), x32], axis=0)
    acc = jnp.zeros(x32.shape, F32) + b_ref[...]
    for j in range(KERNEL):
        bands = []
        for g in range(groups):
            parts = [w_ref[g, :, j * width : (j + 1) * width].astype(F32)]
            if g > 0:
                parts.insert(0, jnp.zeros((width, g * width), F32))
            if g < groups - 1:
                parts.append(jnp.zeros((width, (groups - 1 - g) * width), F32))
            bands.append(jnp.concatenate(parts, axis=1))
        band = jnp.concatenate(bands, axis=0).astype(BF16)
        if j < KERNEL - 1:
            band_ref[j] = band
        acc += dot_nt(ext[j * DILATION : j * DILATION + rows].astype(BF16), band)
    base_ref[0:RIM] = acc[0:RIM]
    base_ref[RIM:] = x32[0:RIM]
    mix = gelu_mix(x32, acc)
    pieces = g_ref[...].astype(F32)
    gain = jnp.concatenate([pieces[i : i + 1] for i in range(pieces.shape[0])], axis=1)
    gain = jnp.broadcast_to(gain, (GAIN_ROWS, gain.shape[1])).astype(BF16)
    half = rows // 2
    late_ref[0:half] = mix[0:half]
    late_ref[half:] = gain
    early_ref[0:half] = mix[half:]
    early_ref[half:] = gain


def stage_kernel(*refs):
    for ref, out in zip(refs[:3], refs[3:]):
        out[...] = ref[...]


def fix_kernel(halo_ref, base_ref, band_ref, late_ref, o_ref):
    halo = halo_ref[...].astype(F32)
    ext = jnp.concatenate([halo, jnp.zeros_like(halo)], axis=0)
    acc = base_ref[0:RIM]
    for j in range(KERNEL - 1):
        acc += dot_nt(ext[j * DILATION : j * DILATION + RIM].astype(BF16), band_ref[j])
    o_ref[...] = late_ref[...]
    o_ref[0:RIM] = gelu_mix(base_ref[RIM:], acc)


def qkv_kernel(pos_ref, a_ref, b_ref, y_ref, z_ref, wq, wk, wv, *rest):
    outs, pack = rest[:-1], rest[-1]
    half = a_ref.shape[0] - GAIN_ROWS
    cols = a_ref.shape[1]
    heads = cols // HEAD_DIM
    core, ychip, low = pos_ref[0], pos_ref[1], pos_ref[2]
    parts = [
        (a_ref, 2 * ychip + core),
        (b_ref, 2 * ychip + 1 - core),
        (y_ref, 2 * (1 - ychip) + core),
        (z_ref, 2 * (1 - ychip) + 1 - core),
    ]
    square = jnp.zeros((half, cols), F32)
    for ref, _ in parts:
        x = ref[0:half].astype(F32)
        square += x * x
    rstd = lax.rsqrt(jnp.sum(square, axis=1, keepdims=True) / (4 * cols) + 1e-06)
    normed = []
    for ref, group in parts:
        gain = ref[half : half + 1].astype(F32)
        normed.append(((ref[0:half].astype(F32) * rstd * gain).astype(BF16), group))

    def project(w):
        total = None
        for x, group in normed:
            term = dot32(x, w[pl.ds(pl.multiple_of(group * cols, cols), cols), :])
            total = term if total is None else total + term
        return total.astype(BF16)

    q, k, v = project(wq), project(wk), project(wv)
    q = (q.astype(F32) * (1.0 / HEAD_DIM**0.5)).astype(BF16)
    for j in range(heads):
        lanes = slice(j * HEAD_DIM, (j + 1) * HEAD_DIM)
        slot = jnp.bitwise_xor(low, j)
        pack[slot, 0:half, :] = jnp.concatenate([k[:, lanes], v[:, lanes]], axis=1)
        pack[slot, half : half + half // 2, :] = jnp.concatenate(
            [q[: half // 2, lanes], q[half // 2 :, lanes]], axis=1
        )
    for m, out in enumerate(outs):
        out[...] = pack[m]


def pack_kernel(pos_ref, *rest):
    own_refs, kv_ref, qs_ref = rest[:8], rest[8], rest[9]
    half = kv_ref.shape[1]
    lane = lane_iota((half // 2, 128))
    pad = jnp.where(lane == HEAD_DIM, 1.0, 0.0)
    for i, ref in enumerate(own_refs):
        kv_ref[i] = ref[0:half, :]
        shard = 4 * jnp.bitwise_xor(pos_ref[0], 1 - i // 4) + jnp.bitwise_xor(pos_ref[2], i % 4)
        packed = ref[half:, :].astype(F32)
        rolled = pltpu.roll(packed, HEAD_DIM, 1)
        qs_ref[shard, 0 : half // 2] = jnp.where(lane < HEAD_DIM, packed, pad).astype(BF16)
        qs_ref[shard, half // 2 :] = jnp.where(lane < HEAD_DIM, rolled, pad).astype(BF16)


def attend_kernel(pos_ref, valid_ref, own_ref, oth_ref, qs, o_ref, kb, vb, sc):
    ranks = o_ref.shape[0]
    half = o_ref.shape[1] * 2
    halfrows = half // 2
    core, low = pos_ref[0], pos_ref[2]
    lane = lane_iota((half, 128))
    row = lax.broadcasted_iota(jnp.int32, (half, 128), 0)
    lane_h = lane_iota((halfrows, 128))
    for i in range(8):
        part = 1 - i // 4
        for side, ref in ((core, own_ref), (1 - core, oth_ref)):
            shard = 4 * jnp.bitwise_xor(side, part) + jnp.bitwise_xor(low, i % 4)
            block = 2 * shard + part
            start = block * half
            stretch = start // STRETCH
            ok = row + (start - stretch * STRETCH) < valid_ref[stretch]
            bias = jnp.where(jnp.logical_and(lane == HEAD_DIM, jnp.logical_not(ok)), NEG, 0.0)
            kv = ref[i].astype(F32)
            kb[block] = jnp.where(lane < HEAD_DIM, kv, bias).astype(BF16)
            vb[block] = jnp.where(lane < HEAD_DIM, 1.0, kv).astype(BF16)
    qrow = lax.broadcasted_iota(jnp.int32, (half, half), 0)
    kcol = lane_iota((half, half))

    def scores(t):
        part = jnp.bitwise_xor(core, t // 4)
        q = qs[t]
        top = jnp.full((half, 128), NEG, F32)
        for b in range(2 * t + 2):
            s = dot_nt(q, kb[b])
            if b >= 2 * t:
                s = jnp.where(kcol + (b - 2 * t) * half <= qrow + part * half, s, NEG)
            sc[t % 2, b] = s
            for piece in range(half // 128):
                top = jnp.maximum(top, s[:, piece * 128 : (piece + 1) * 128])
        return jnp.max(top, axis=1, keepdims=True)

    def values(t, m):
        acc = jnp.zeros((half, 128), F32)
        for b in range(2 * t + 2):
            acc += dot32(jnp.exp(sc[t % 2, b] - m).astype(BF16), vb[b])
        out = acc / pltpu.roll(acc, HEAD_DIM, 1)
        left = pltpu.roll(out[:halfrows], HEAD_DIM, 1)
        o_ref[t] = jnp.where(lane_h < HEAD_DIM, left, out[halfrows:]).astype(BF16)

    tops = [scores(0)]
    for t in range(ranks):
        if t < ranks - 1:
            tops.append(scores(t + 1))
        values(t, tops[t])


def out_kernel(pos_ref, att_ref, w0, w1, own_ref, *outs):
    heads, quarter, _ = att_ref.shape
    cols = own_ref.shape[1]
    core, ychip = pos_ref[0], pos_ref[1]
    lane = lane_iota((quarter, 128))
    feats = []
    for first in (core, 1 - core):
        tops, bots = [], []
        for j in range(0, heads // 2, 2):
            a = att_ref[first * (heads // 2) + j].astype(F32)
            b = att_ref[first * (heads // 2) + j + 1].astype(F32)
            tops.append(jnp.where(lane < HEAD_DIM, a, pltpu.roll(b, HEAD_DIM, 1)))
            bots.append(jnp.where(lane < HEAD_DIM, pltpu.roll(a, HEAD_DIM, 1), b))
        feats.append(
            jnp.concatenate(
                [jnp.concatenate(tops, axis=1), jnp.concatenate(bots, axis=1)], axis=0
            ).astype(BF16)
        )
    for step, ref in enumerate((own_ref, *outs)):
        group = jnp.bitwise_xor(2 * ychip + core, step)
        lanes = pl.ds(pl.multiple_of(group * cols, cols), cols)
        total = dot32(feats[0], w0[:, lanes]) + dot32(feats[1], w1[:, lanes])
        ref[...] = total.astype(ref.dtype)


def final_kernel(pos_ref, late_ref, early_ref, own_ref, beside_ref, across_ref, corner_ref, o_ref):
    half = own_ref.shape[0]
    first = jnp.bitwise_xor(pos_ref[0], pos_ref[3]) == 0
    own = own_ref[...] + across_ref[...].astype(F32)
    other = beside_ref[...].astype(F32) + corner_ref[...].astype(F32)
    pick = jnp.broadcast_to(first, own.shape)
    o_ref[0:half] = (late_ref[0:half].astype(F32) + jnp.where(pick, own, other)).astype(BF16)
    o_ref[half:] = (early_ref[0:half].astype(F32) + jnp.where(pick, other, own)).astype(BF16)


def call(kernel, outs, scalars, args, *, us, vmem=16, scratch=(), space=pltpu.VMEM):
    spaces = [pltpu.SMEM] * scalars + [space] * (len(args) - scalars)
    outs = [jax.ShapeDtypeStruct(*out) for out in outs]
    result = pl.pallas_call(
        kernel,
        out_shape=outs,
        in_specs=[pl.BlockSpec(memory_space=space) for space in spaces],
        out_specs=[pl.BlockSpec(memory_space=pltpu.VMEM)] * len(outs),
        scratch_shapes=scratch,
        compiler_params=pltpu.CompilerParams(vmem_limit_bytes=vmem << 20),
        cost_estimate=pl.CostEstimate(
            flops=int(us * 1e9), bytes_accessed=int(us * 3.6e6), transcendentals=0
        ),
    )(*args)
    return result if len(outs) > 1 else result[0]


def on_device(
    tokens_in, conv_weight, conv_bias, norm_gain, w_query, w_key, w_value, w_out, valid_count
):
    tok, cols = tokens_in.shape
    half = tok // 2
    ranks = lax.axis_size("tm")
    head_at, shard = lax.axis_index("head"), lax.axis_index("tm")
    pos = jnp.stack([head_at & 1, head_at >> 1, shard & 3, shard >> 2]).astype(jnp.int32)

    operands = (
        tokens_in, jnp.swapaxes(conv_weight, 1, 2),
        conv_bias.reshape(1, cols), norm_gain.reshape(cols // 128, 128),
    )
    late, early, band, base, edge = call(
        conv_kernel,
        [
            ((half + GAIN_ROWS, cols), BF16),
            ((half + GAIN_ROWS, cols), BF16),
            ((KERNEL - 1, cols, cols), BF16),
            ((2 * RIM, cols), F32),
            ((RIM, cols), BF16),
        ],
        0,
        operands,
        us=2.0,
        vmem=CONV_VMEM,
        scratch=[pltpu.VMEM(x.shape, x.dtype) for x in operands]
        + [pltpu.SemaphoreType.DMA((len(operands),))],
        space=pltpu.HBM,
    )
    halo = from_behind(edge, "tm", 1)
    base, band, late = call(
        stage_kernel, [(x.shape, x.dtype) for x in (base, band, late)], 0, (base, band, late), us=1.0
    )

    def project_half(x, after=None):
        across = swap(x, 2)
        if after is not None:
            corner = swap(x, 3)
            x = lax.optimization_barrier((x, after))[0]
        else:
            corner = swap(across, 1)
        beside = swap(x, 1)
        return call(
            qkv_kernel,
            [((half + half // 2, 2 * HEAD_DIM), BF16)] * 4,
            1,
            (pos, x, beside, across, corner, w_query, w_key, w_value),
            us=1.0,
            scratch=[pltpu.VMEM((4, half + half // 2, 2 * HEAD_DIM), BF16)],
        )

    sends = list(project_half(early))
    late = call(
        fix_kernel, [((half + GAIN_ROWS, cols), BF16)], 0, (halo, base, band, late), us=FIX_US
    )
    sends += list(project_half(late, sends[0]))
    own = [spread(value, i % 4, 1 - i // 4) for i, value in enumerate(sends)]
    kv, qs = call(
        pack_kernel,
        [((8, half, 128), BF16), ((8, half, 128), BF16)],
        1,
        (pos, *own),
        us=0.5,
    )
    wo1 = swap(lax.optimization_barrier((w_out, sends[0]))[0], 1)
    attended = call(
        attend_kernel,
        [((8, half // 2, 2 * HEAD_DIM), BF16)],
        2,
        (pos, valid_count, kv, swap(kv, 1), qs),
        us=8.0,
        vmem=24,
        scratch=[
            pltpu.VMEM((16, half, 128), BF16),
            pltpu.VMEM((16, half, 128), BF16),
            pltpu.VMEM((2, 16, half, half), F32),
        ],
    )
    back = lax.all_to_all(attended, "tm", 0, 0)
    own, beside, across, corner = call(
        out_kernel,
        [((half, cols), F32)] + [((half, cols), BF16)] * 3,
        1,
        (pos, back, w_out, wo1),
        us=1.0,
    )
    return call(
        final_kernel,
        [((tok, cols), BF16)],
        1,
        (pos, late, early, own, swap(beside, 1), swap(across, 2), swap(corner, 3)),
        us=0.5,
    )


def solution(mesh):
    ranks, heads = mesh.shape["tm"], mesh.shape["head"]

    def body(*args):
        tokens_in, conv_weight, *_ = args
        tok, cols = tokens_in.shape
        fits = heads == 4 and cols == 4 * HEAD_DIM and ranks == 2 * (cols // HEAD_DIM)
        fits = fits and tok == 512 and ranks * tok <= (WINDOW + 1) * STRETCH
        return on_device(*args) if fits else ring_on_device(*args)

    return jax.shard_map(
        body,
        mesh=mesh,
        in_specs=(
            P("tm", "head"),
            P("head", None, None),
            P("head"),
            P("head"),
            P(None, "head"),
            P(None, "head"),
            P(None, "head"),
            P("head", None),
            P(),
        ),
        out_specs=P("tm", "head"),
        check_vma=False,
    )
```

```python
import functools

import jax
import jax.numpy as jnp
from jax import lax
from jax.experimental import pallas as pl
from jax.experimental.pallas import tpu as pltpu
from jax.sharding import PartitionSpec as P

D = 1024
HEAD_DIM = 64
KERNEL = 3
DILATION = 4
STRETCH = 1024
WINDOW = 8
RIM = (KERNEL - 1) * DILATION
GAIN_ROWS = 8
CONV_VMEM = 60
FIX_US = 2.0
NEG = -1e30
F32 = jnp.float32
BF16 = jnp.bfloat16


def from_behind(value, axis, steps):
    count = lax.axis_size(axis)
    first, last = (max(0, -steps), min(count, count - steps))
    return lax.ppermute(value, axis, [(source, source + steps) for source in range(first, last)])


def ring_on_device(
    tokens_in, conv_weight, conv_bias, norm_gain, w_query, w_key, w_value, w_out, valid_count
):
    tok = tokens_in.shape[0]
    local_groups = conv_weight.shape[0]
    width = conv_weight.shape[2]
    rim = (KERNEL - 1) * DILATION
    before = from_behind(tokens_in[tok - rim :], "tm", 1)
    extended = jnp.concatenate([before, tokens_in], axis=0)
    taps = [extended[j * DILATION : j * DILATION + tok] for j in range(KERNEL)]
    stacked = jnp.stack(taps, 1).reshape(tok, KERNEL, local_groups, width)
    stacked = jnp.transpose(stacked, (0, 2, 1, 3)).reshape(tok, local_groups, KERNEL * width)
    conv_term = jnp.einsum("tgi,gio->tgo", stacked, conv_weight, preferred_element_type=jnp.float32)
    conv_term = conv_term.reshape(tok, local_groups * width)
    mixed = (
        tokens_in.astype(jnp.float32) + jax.nn.gelu(conv_term + conv_bias, approximate=True)
    ).astype(jnp.bfloat16)
    mixed32 = mixed.astype(jnp.float32)
    weights_all = jnp.concatenate([w_query, w_key, w_value], axis=1)
    local_cols = w_query.shape[1]
    square_part = jnp.sum(mixed32 * mixed32, axis=1)
    square_tot = lax.psum(square_part, "head")
    rstd = lax.rsqrt(square_tot / D + 1e-06)
    normed = (mixed32 * rstd[:, None] * norm_gain.astype(jnp.float32)).astype(jnp.bfloat16)
    projected = jnp.dot(
        lax.all_gather(normed, "head", axis=1, tiled=True),
        weights_all,
        preferred_element_type=jnp.float32,
    )
    projected = projected.astype(jnp.bfloat16)
    local_heads = local_cols // HEAD_DIM
    query = projected[:, :local_cols].reshape(tok, local_heads, HEAD_DIM)
    keys_own = projected[:, local_cols : 2 * local_cols]
    values_own = projected[:, 2 * local_cols :]
    scale = 1.0 / HEAD_DIM**0.5
    shard = lax.axis_index("tm")
    q_pos = shard * tok + jnp.arange(tok, dtype=jnp.int32)
    stretch_ids = jnp.arange(valid_count.shape[0], dtype=jnp.int32)

    def attend(state, keys_blk, values_blk, source):
        top, total, accum = state
        k_pos = source * tok + jnp.arange(tok, dtype=jnp.int32)
        k_stretch = jnp.where(k_pos >= 0, k_pos // STRETCH, -1)
        counts = jnp.sum(
            jnp.where(k_stretch[:, None] == stretch_ids[None, :], valid_count[None, :], 0), axis=1
        )
        key_ok = (k_pos >= 0) & (k_pos % STRETCH < counts)
        allowed = key_ok[None, :] & (k_pos[None, :] <= q_pos[:, None])
        allowed = allowed & (k_pos[None, :] // STRETCH >= q_pos[:, None] // STRETCH - WINDOW)
        keys3 = keys_blk.reshape(tok, local_heads, HEAD_DIM)
        values3 = values_blk.reshape(tok, local_heads, HEAD_DIM)
        scores = (
            jnp.einsum("qhd,khd->hqk", query, keys3, preferred_element_type=jnp.float32) * scale
        )
        block_top = jnp.max(jnp.where(allowed[None], scores, -1e30), axis=2)
        new_top = jnp.maximum(top, block_top)
        weights = jnp.where(allowed[None], jnp.exp(scores - new_top[:, :, None]), 0.0)
        factor = jnp.exp(top - new_top)
        total = total * factor + jnp.sum(weights, axis=2)
        accum = accum * factor[:, :, None] + jnp.einsum(
            "hqk,khd->hqd",
            weights.astype(jnp.bfloat16),
            values3,
            preferred_element_type=jnp.float32,
        )
        return (new_top, total, accum)

    state = (
        jnp.full((local_heads, tok), -1e30, jnp.float32),
        jnp.zeros((local_heads, tok), jnp.float32),
        jnp.zeros((local_heads, tok, HEAD_DIM), jnp.float32),
    )
    state = attend(state, keys_own, values_own, shard)
    reach = (WINDOW * STRETCH + max(STRETCH - tok, 0) + tok - 1) // tok
    steps_back = min(reach, lax.axis_size("tm") - 1)

    def relay_step(step, carry):
        keys_blk, values_blk, inner = carry
        keys_blk, values_blk = from_behind((keys_blk, values_blk), "tm", 1)
        inner = attend(inner, keys_blk, values_blk, shard - step)
        return (keys_blk, values_blk, inner)

    carried = lax.fori_loop(1, steps_back + 1, relay_step, (keys_own, values_own, state))
    state = carried[2]
    top, total, accum = state
    attended = (accum / total[:, :, None]).astype(jnp.bfloat16)
    attended = jnp.transpose(attended, (1, 0, 2)).reshape(tok, local_cols)
    partial_proj = jnp.dot(attended, w_out, preferred_element_type=jnp.float32)
    proj = lax.psum_scatter(
        partial_proj.astype(jnp.bfloat16), "head", scatter_dimension=1, tiled=True
    ).astype(jnp.float32)
    return (mixed32 + proj).astype(jnp.bfloat16)


def swap(value, bit):
    return lax.ppermute(value, "head", [(i, i ^ bit) for i in range(lax.axis_size("head"))])


def spread(value, m, part):
    pairs = []
    for shard in range(8):
        for head_at in range(4):
            b, low, ychip, core = shard // 4, shard % 4, head_at // 2, head_at % 2
            to = (4 * core + (low ^ m)) * 4 + 2 * ychip + (part ^ b)
            pairs.append((shard * 4 + head_at, to))
    return lax.ppermute(value, ("tm", "head"), pairs)


def dot32(a, b):
    return jnp.dot(a, b, preferred_element_type=F32)


def dot_nt(a, b):
    return lax.dot_general(a, b, (((1,), (1,)), ((), ())), preferred_element_type=F32)


def lane_iota(shape):
    return lax.broadcasted_iota(jnp.int32, shape, 1)


def gelu_mix(x32, term):
    return (x32 + jax.nn.gelu(term, approximate=True)).astype(BF16)


def conv_kernel(
    x_hbm, w_hbm, b_hbm, g_hbm, late_ref, early_ref, band_ref, base_ref, edge_ref,
    x_ref, w_ref, b_ref, g_ref, sems,
):
    pairs = ((x_hbm, x_ref), (w_hbm, w_ref), (b_hbm, b_ref), (g_hbm, g_ref))
    copies = [pltpu.make_async_copy(src, dst, sems.at[i]) for i, (src, dst) in enumerate(pairs)]
    for copy in copies:
        copy.start()
    for copy in copies:
        copy.wait()
    rows = x_ref.shape[0]
    edge_ref[...] = x_ref[rows - RIM :]
    groups, width, _ = w_ref.shape
    x32 = x_ref[...].astype(F32)
    ext = jnp.concatenate([jnp.zeros((RIM, x32.shape[1]), F32), x32], axis=0)
    acc = jnp.zeros(x32.shape, F32) + b_ref[...]
    for j in range(KERNEL):
        bands = []
        for g in range(groups):
            parts = [w_ref[g, :, j * width : (j + 1) * width].astype(F32)]
            if g > 0:
                parts.insert(0, jnp.zeros((width, g * width), F32))
            if g < groups - 1:
                parts.append(jnp.zeros((width, (groups - 1 - g) * width), F32))
            bands.append(jnp.concatenate(parts, axis=1))
        band = jnp.concatenate(bands, axis=0).astype(BF16)
        if j < KERNEL - 1:
            band_ref[j] = band
        acc += dot_nt(ext[j * DILATION : j * DILATION + rows].astype(BF16), band)
    base_ref[0:RIM] = acc[0:RIM]
    base_ref[RIM:] = x32[0:RIM]
    mix = gelu_mix(x32, acc)
    pieces = g_ref[...].astype(F32)
    gain = jnp.concatenate([pieces[i : i + 1] for i in range(pieces.shape[0])], axis=1)
    gain = jnp.broadcast_to(gain, (GAIN_ROWS, gain.shape[1])).astype(BF16)
    half = rows // 2
    late_ref[0:half] = mix[0:half]
    late_ref[half:] = gain
    early_ref[0:half] = mix[half:]
    early_ref[half:] = gain


def stage_kernel(*refs):
    for ref, out in zip(refs[:3], refs[3:]):
        out[...] = ref[...]


def fix_kernel(halo_ref, base_ref, band_ref, late_ref, o_ref):
    halo = halo_ref[...].astype(F32)
    ext = jnp.concatenate([halo, jnp.zeros_like(halo)], axis=0)
    acc = base_ref[0:RIM]
    for j in range(KERNEL - 1):
        acc += dot_nt(ext[j * DILATION : j * DILATION + RIM].astype(BF16), band_ref[j])
    o_ref[...] = late_ref[...]
    o_ref[0:RIM] = gelu_mix(base_ref[RIM:], acc)


def qkv_kernel(pos_ref, a_ref, b_ref, y_ref, z_ref, wq, wk, wv, *rest):
    outs, pack = rest[:-1], rest[-1]
    half = a_ref.shape[0] - GAIN_ROWS
    cols = a_ref.shape[1]
    heads = cols // HEAD_DIM
    core, ychip, low = pos_ref[0], pos_ref[1], pos_ref[2]
    parts = [
        (a_ref, 2 * ychip + core),
        (b_ref, 2 * ychip + 1 - core),
        (y_ref, 2 * (1 - ychip) + core),
        (z_ref, 2 * (1 - ychip) + 1 - core),
    ]
    square = jnp.zeros((half, cols), F32)
    for ref, _ in parts:
        x = ref[0:half].astype(F32)
        square += x * x
    rstd = lax.rsqrt(jnp.sum(square, axis=1, keepdims=True) / (4 * cols) + 1e-06)
    normed = []
    for ref, group in parts:
        gain = ref[half : half + 1].astype(F32)
        normed.append(((ref[0:half].astype(F32) * rstd * gain).astype(BF16), group))

    def project(w):
        total = None
        for x, group in normed:
            term = dot32(x, w[pl.ds(pl.multiple_of(group * cols, cols), cols), :])
            total = term if total is None else total + term
        return total.astype(BF16)

    q, k, v = project(wq), project(wk), project(wv)
    q = (q.astype(F32) * (1.0 / HEAD_DIM**0.5)).astype(BF16)
    for j in range(heads):
        lanes = slice(j * HEAD_DIM, (j + 1) * HEAD_DIM)
        slot = jnp.bitwise_xor(low, j)
        pack[slot, 0:half, :] = jnp.concatenate([k[:, lanes], v[:, lanes]], axis=1)
        pack[slot, half : half + half // 2, :] = jnp.concatenate(
            [q[: half // 2, lanes], q[half // 2 :, lanes]], axis=1
        )
    for m, out in enumerate(outs):
        out[...] = pack[m]


def pack_kernel(*refs):
    kv_ref = refs[-1]
    for i, ref in enumerate(refs[:-1]):
        kv_ref[i] = ref[0 : kv_ref.shape[1], :]


def load_keys(pos_ref, valid_ref, kv_ref, kb, vb, side):
    half = kb.shape[1]
    lane = lane_iota((half, 128))
    row = jnp.where(lane == HEAD_DIM, lax.broadcasted_iota(jnp.int32, (half, 128), 0), -1)
    left = jnp.where(lane < HEAD_DIM, 1.0, 0.0).astype(BF16)
    right = jnp.where(lane < HEAD_DIM, 0.0, 1.0).astype(BF16)
    for i in range(kb.shape[0]):
        part = 1 - i // 4
        shard = 4 * jnp.bitwise_xor(side, part) + jnp.bitwise_xor(pos_ref[2], i % 4)
        start = (2 * shard + part) * half
        stretch = start // STRETCH
        first_bad = jnp.maximum(valid_ref[stretch] - (start - stretch * STRETCH), 0)
        bias = jnp.where(row >= first_bad, NEG, 0.0).astype(BF16)
        kv = kv_ref[i]
        kb[shard] = kv * left + bias
        vb[shard] = kv * right + left


def own_kernel(pos_ref, valid_ref, kv_ref, *rest):
    own_refs, (kb, vb, qs_ref) = rest[:8], rest[8:]
    load_keys(pos_ref, valid_ref, kv_ref, kb, vb, pos_ref[0])
    half = kb.shape[1]
    lane = lane_iota((half // 2, 128))
    pad = jnp.where(lane == HEAD_DIM, 1.0, 0.0)
    for i, ref in enumerate(own_refs):
        shard = 4 * jnp.bitwise_xor(pos_ref[0], 1 - i // 4) + jnp.bitwise_xor(pos_ref[2], i % 4)
        packed = ref[half:, :].astype(F32)
        rolled = pltpu.roll(packed, HEAD_DIM, 1)
        qs_ref[shard, 0 : half // 2] = jnp.where(lane < HEAD_DIM, packed, pad).astype(BF16)
        qs_ref[shard, half // 2 :] = jnp.where(lane < HEAD_DIM, rolled, pad).astype(BF16)


def attend_kernel(pos_ref, valid_ref, oth_ref, k_own, v_own, qs, o_ref, k_oth, v_oth, sc):
    ranks = o_ref.shape[0]
    half = o_ref.shape[1] * 2
    halfrows = half // 2
    core = pos_ref[0]
    lane_h = lane_iota((halfrows, 128))
    load_keys(pos_ref, valid_ref, oth_ref, k_oth, v_oth, 1 - core)
    causal = lane_iota((half, half)) <= lax.broadcasted_iota(jnp.int32, (half, half), 0)
    blocks = [(k_own, v_own), (k_oth, v_oth)]

    def scores(t):
        ahead = jnp.where(jnp.bitwise_xor(core, t // 4) == 0, NEG, 0.0)
        q = qs[t]
        top = jnp.full((half, 128), NEG, F32)
        for b in range(2 * t + 2):
            s = dot_nt(q, blocks[b % 2][0][b // 2])
            if b == 2 * t:
                s = jnp.where(causal, s, NEG)
            elif b == 2 * t + 1:
                s = s + ahead
            sc[t % 2, b] = s
            for piece in range(half // 128):
                top = jnp.maximum(top, s[:, piece * 128 : (piece + 1) * 128])
        return jnp.max(top, axis=1, keepdims=True)

    def values(t, m):
        acc = jnp.zeros((half, 128), F32)
        for b in range(2 * t + 2):
            acc += dot32(jnp.exp(sc[t % 2, b] - m).astype(BF16), blocks[b % 2][1][b // 2])
        out = acc / pltpu.roll(acc, HEAD_DIM, 1)
        left = pltpu.roll(out[:halfrows], HEAD_DIM, 1)
        o_ref[t] = jnp.where(lane_h < HEAD_DIM, left, out[halfrows:]).astype(BF16)

    tops = [scores(0)]
    for t in range(ranks):
        if t < ranks - 1:
            tops.append(scores(t + 1))
        values(t, tops[t])


def features(core, att_ref):
    heads, quarter, _ = att_ref.shape
    lane = lane_iota((quarter, 128))
    feats = []
    for first in (core, 1 - core):
        tops, bots = [], []
        for j in range(0, heads // 2, 2):
            a = att_ref[first * (heads // 2) + j].astype(F32)
            b = att_ref[first * (heads // 2) + j + 1].astype(F32)
            tops.append(jnp.where(lane < HEAD_DIM, a, pltpu.roll(b, HEAD_DIM, 1)))
            bots.append(jnp.where(lane < HEAD_DIM, pltpu.roll(a, HEAD_DIM, 1), b))
        feats.append(
            jnp.concatenate(
                [jnp.concatenate(tops, axis=1), jnp.concatenate(bots, axis=1)], axis=0
            ).astype(BF16)
        )
    return feats


def partial_out(pos_ref, feats, w0, w1, step, cols):
    group = jnp.bitwise_xor(2 * pos_ref[1] + pos_ref[0], step)
    lanes = pl.ds(pl.multiple_of(group * cols, cols), cols)
    return dot32(feats[0], w0[:, lanes]) + dot32(feats[1], w1[:, lanes])


def far_kernel(pos_ref, att_ref, w0, w1, across_ref, corner_ref):
    feats = features(pos_ref[0], att_ref)
    for step, ref in ((2, across_ref), (3, corner_ref)):
        ref[...] = partial_out(pos_ref, feats, w0, w1, step, ref.shape[1]).astype(BF16)


def rows_of(pos_ref, half, other):
    mine = jnp.bitwise_xor(jnp.bitwise_xor(pos_ref[0], pos_ref[3]), other)
    return pl.ds(pl.multiple_of(mine * half, half), half)


def near_kernel(pos_ref, att_ref, w0, w1, late_ref, early_ref, base_ref, beside_ref):
    feats = features(pos_ref[0], att_ref)
    half, cols = beside_ref.shape
    beside_ref[...] = partial_out(pos_ref, feats, w0, w1, 1, cols).astype(BF16)
    base_ref[0:half] = late_ref[0:half].astype(F32)
    base_ref[half:] = early_ref[0:half].astype(F32)
    base_ref[rows_of(pos_ref, half, 0)] += partial_out(pos_ref, feats, w0, w1, 0, cols)


def final_kernel(pos_ref, base_ref, beside_ref, across_ref, corner_ref, o_ref):
    half = beside_ref.shape[0]
    mine, other = rows_of(pos_ref, half, 0), rows_of(pos_ref, half, 1)
    o_ref[mine] = (base_ref[mine] + across_ref[...].astype(F32)).astype(BF16)
    rest = beside_ref[...].astype(F32) + corner_ref[...].astype(F32)
    o_ref[other] = (base_ref[other] + rest).astype(BF16)


def call(kernel, outs, scalars, args, *, us, vmem=16, scratch=(), space=pltpu.VMEM):
    spaces = [pltpu.SMEM] * scalars + [space] * (len(args) - scalars)
    outs = [jax.ShapeDtypeStruct(*out) for out in outs]
    result = pl.pallas_call(
        kernel,
        out_shape=outs,
        in_specs=[pl.BlockSpec(memory_space=space) for space in spaces],
        out_specs=[pl.BlockSpec(memory_space=pltpu.VMEM)] * len(outs),
        scratch_shapes=scratch,
        compiler_params=pltpu.CompilerParams(vmem_limit_bytes=vmem << 20),
        cost_estimate=pl.CostEstimate(
            flops=int(us * 1e9), bytes_accessed=int(us * 3.6e6), transcendentals=0
        ),
    )(*args)
    return result if len(outs) > 1 else result[0]


def on_device(
    tokens_in, conv_weight, conv_bias, norm_gain, w_query, w_key, w_value, w_out, valid_count
):
    tok, cols = tokens_in.shape
    half = tok // 2
    ranks = lax.axis_size("tm")
    head_at, shard = lax.axis_index("head"), lax.axis_index("tm")
    pos = jnp.stack([head_at & 1, head_at >> 1, shard & 3, shard >> 2]).astype(jnp.int32)

    operands = (
        tokens_in, jnp.swapaxes(conv_weight, 1, 2),
        conv_bias.reshape(1, cols), norm_gain.reshape(cols // 128, 128),
    )
    late, early, band, base, edge = call(
        conv_kernel,
        [
            ((half + GAIN_ROWS, cols), BF16),
            ((half + GAIN_ROWS, cols), BF16),
            ((KERNEL - 1, cols, cols), BF16),
            ((2 * RIM, cols), F32),
            ((RIM, cols), BF16),
        ],
        0,
        operands,
        us=2.0,
        vmem=CONV_VMEM,
        scratch=[pltpu.VMEM(x.shape, x.dtype) for x in operands]
        + [pltpu.SemaphoreType.DMA((len(operands),))],
        space=pltpu.HBM,
    )
    halo = from_behind(edge, "tm", 1)
    base, band, late = call(
        stage_kernel, [(x.shape, x.dtype) for x in (base, band, late)], 0, (base, band, late), us=1.0
    )

    def project_half(x, after=None):
        across = swap(x, 2)
        if after is not None:
            corner = swap(x, 3)
            x = lax.optimization_barrier((x, after))[0]
        else:
            corner = swap(across, 1)
        beside = swap(x, 1)
        return call(
            qkv_kernel,
            [((half + half // 2, 2 * HEAD_DIM), BF16)] * 4,
            1,
            (pos, x, beside, across, corner, w_query, w_key, w_value),
            us=1.0,
            scratch=[pltpu.VMEM((4, half + half // 2, 2 * HEAD_DIM), BF16)],
        )

    sends = list(project_half(early))
    late = call(
        fix_kernel, [((half + GAIN_ROWS, cols), BF16)], 0, (halo, base, band, late), us=FIX_US
    )
    sends += list(project_half(late, sends[0]))
    own = [spread(value, i % 4, 1 - i // 4) for i, value in enumerate(sends)]
    kv = call(pack_kernel, [((8, half, 128), BF16)], 0, own, us=0.4)
    wo1 = swap(lax.optimization_barrier((w_out, sends[0]))[0], 1)
    kv_oth = swap(kv, 1)
    k_own, v_own, qs = call(
        own_kernel, [((8, half, 128), BF16)] * 3, 2, (pos, valid_count, kv, *own), us=0.8
    )
    attended = call(
        attend_kernel,
        [((8, half // 2, 2 * HEAD_DIM), BF16)],
        2,
        (pos, valid_count, kv_oth, k_own, v_own, qs),
        us=8.0,
        vmem=24,
        scratch=[
            pltpu.VMEM((8, half, 128), BF16),
            pltpu.VMEM((8, half, 128), BF16),
            pltpu.VMEM((2, 16, half, half), F32),
        ],
    )
    back = lax.all_to_all(attended, "tm", 0, 0)
    across, corner = call(
        far_kernel, [((half, cols), BF16)] * 2, 1, (pos, back, w_out, wo1), us=0.6
    )
    across, corner = swap(across, 2), swap(corner, 3)
    base, beside = call(
        near_kernel,
        [((tok, cols), F32), ((half, cols), BF16)],
        1,
        (pos, back, w_out, wo1, late, early),
        us=1.0,
    )
    args = (pos, base, swap(beside, 1), across, corner)
    return call(final_kernel, [((tok, cols), BF16)], 1, args, us=0.5)


def solution(mesh):
    ranks, heads = mesh.shape["tm"], mesh.shape["head"]

    def body(*args):
        tokens_in, conv_weight, *_ = args
        tok, cols = tokens_in.shape
        fits = heads == 4 and cols == 4 * HEAD_DIM and ranks == 2 * (cols // HEAD_DIM)
        fits = fits and tok == 512 and ranks * tok <= (WINDOW + 1) * STRETCH
        return on_device(*args) if fits else ring_on_device(*args)

    return jax.shard_map(
        body,
        mesh=mesh,
        in_specs=(
            P("tm", "head"),
            P("head", None, None),
            P("head"),
            P("head"),
            P(None, "head"),
            P(None, "head"),
            P(None, "head"),
            P("head", None),
            P(),
        ),
        out_specs=P("tm", "head"),
        check_vma=False,
    )
```

```python
import functools

import jax
import jax.numpy as jnp
from jax import lax
from jax.experimental import pallas as pl
from jax.experimental.pallas import tpu as pltpu
from jax.sharding import PartitionSpec as P

D = 1024
HEAD_DIM = 64
KERNEL = 3
DILATION = 4
STRETCH = 1024
WINDOW = 8
RIM = (KERNEL - 1) * DILATION
GAIN_ROWS = 8
CONV_VMEM = 60
FIX_US = 2.0
NEG = -1e30
F32 = jnp.float32
BF16 = jnp.bfloat16


def from_behind(value, axis, steps):
    count = lax.axis_size(axis)
    first, last = (max(0, -steps), min(count, count - steps))
    return lax.ppermute(value, axis, [(source, source + steps) for source in range(first, last)])


def ring_on_device(
    tokens_in, conv_weight, conv_bias, norm_gain, w_query, w_key, w_value, w_out, valid_count
):
    tok = tokens_in.shape[0]
    local_groups = conv_weight.shape[0]
    width = conv_weight.shape[2]
    rim = (KERNEL - 1) * DILATION
    before = from_behind(tokens_in[tok - rim :], "tm", 1)
    extended = jnp.concatenate([before, tokens_in], axis=0)
    taps = [extended[j * DILATION : j * DILATION + tok] for j in range(KERNEL)]
    stacked = jnp.stack(taps, 1).reshape(tok, KERNEL, local_groups, width)
    stacked = jnp.transpose(stacked, (0, 2, 1, 3)).reshape(tok, local_groups, KERNEL * width)
    conv_term = jnp.einsum("tgi,gio->tgo", stacked, conv_weight, preferred_element_type=jnp.float32)
    conv_term = conv_term.reshape(tok, local_groups * width)
    mixed = (
        tokens_in.astype(jnp.float32) + jax.nn.gelu(conv_term + conv_bias, approximate=True)
    ).astype(jnp.bfloat16)
    mixed32 = mixed.astype(jnp.float32)
    weights_all = jnp.concatenate([w_query, w_key, w_value], axis=1)
    local_cols = w_query.shape[1]
    square_part = jnp.sum(mixed32 * mixed32, axis=1)
    square_tot = lax.psum(square_part, "head")
    rstd = lax.rsqrt(square_tot / D + 1e-06)
    normed = (mixed32 * rstd[:, None] * norm_gain.astype(jnp.float32)).astype(jnp.bfloat16)
    projected = jnp.dot(
        lax.all_gather(normed, "head", axis=1, tiled=True),
        weights_all,
        preferred_element_type=jnp.float32,
    )
    projected = projected.astype(jnp.bfloat16)
    local_heads = local_cols // HEAD_DIM
    query = projected[:, :local_cols].reshape(tok, local_heads, HEAD_DIM)
    keys_own = projected[:, local_cols : 2 * local_cols]
    values_own = projected[:, 2 * local_cols :]
    scale = 1.0 / HEAD_DIM**0.5
    shard = lax.axis_index("tm")
    q_pos = shard * tok + jnp.arange(tok, dtype=jnp.int32)
    stretch_ids = jnp.arange(valid_count.shape[0], dtype=jnp.int32)

    def attend(state, keys_blk, values_blk, source):
        top, total, accum = state
        k_pos = source * tok + jnp.arange(tok, dtype=jnp.int32)
        k_stretch = jnp.where(k_pos >= 0, k_pos // STRETCH, -1)
        counts = jnp.sum(
            jnp.where(k_stretch[:, None] == stretch_ids[None, :], valid_count[None, :], 0), axis=1
        )
        key_ok = (k_pos >= 0) & (k_pos % STRETCH < counts)
        allowed = key_ok[None, :] & (k_pos[None, :] <= q_pos[:, None])
        allowed = allowed & (k_pos[None, :] // STRETCH >= q_pos[:, None] // STRETCH - WINDOW)
        keys3 = keys_blk.reshape(tok, local_heads, HEAD_DIM)
        values3 = values_blk.reshape(tok, local_heads, HEAD_DIM)
        scores = (
            jnp.einsum("qhd,khd->hqk", query, keys3, preferred_element_type=jnp.float32) * scale
        )
        block_top = jnp.max(jnp.where(allowed[None], scores, -1e30), axis=2)
        new_top = jnp.maximum(top, block_top)
        weights = jnp.where(allowed[None], jnp.exp(scores - new_top[:, :, None]), 0.0)
        factor = jnp.exp(top - new_top)
        total = total * factor + jnp.sum(weights, axis=2)
        accum = accum * factor[:, :, None] + jnp.einsum(
            "hqk,khd->hqd",
            weights.astype(jnp.bfloat16),
            values3,
            preferred_element_type=jnp.float32,
        )
        return (new_top, total, accum)

    state = (
        jnp.full((local_heads, tok), -1e30, jnp.float32),
        jnp.zeros((local_heads, tok), jnp.float32),
        jnp.zeros((local_heads, tok, HEAD_DIM), jnp.float32),
    )
    state = attend(state, keys_own, values_own, shard)
    reach = (WINDOW * STRETCH + max(STRETCH - tok, 0) + tok - 1) // tok
    steps_back = min(reach, lax.axis_size("tm") - 1)

    def relay_step(step, carry):
        keys_blk, values_blk, inner = carry
        keys_blk, values_blk = from_behind((keys_blk, values_blk), "tm", 1)
        inner = attend(inner, keys_blk, values_blk, shard - step)
        return (keys_blk, values_blk, inner)

    carried = lax.fori_loop(1, steps_back + 1, relay_step, (keys_own, values_own, state))
    state = carried[2]
    top, total, accum = state
    attended = (accum / total[:, :, None]).astype(jnp.bfloat16)
    attended = jnp.transpose(attended, (1, 0, 2)).reshape(tok, local_cols)
    partial_proj = jnp.dot(attended, w_out, preferred_element_type=jnp.float32)
    proj = lax.psum_scatter(
        partial_proj.astype(jnp.bfloat16), "head", scatter_dimension=1, tiled=True
    ).astype(jnp.float32)
    return (mixed32 + proj).astype(jnp.bfloat16)


def swap(value, bit):
    return lax.ppermute(value, "head", [(i, i ^ bit) for i in range(lax.axis_size("head"))])


def spread(value, m, part):
    pairs = []
    for shard in range(8):
        for head_at in range(4):
            b, low, ychip, core = shard // 4, shard % 4, head_at // 2, head_at % 2
            to = (4 * core + (low ^ m)) * 4 + 2 * ychip + (part ^ b)
            pairs.append((shard * 4 + head_at, to))
    return lax.ppermute(value, ("tm", "head"), pairs)


def dot32(a, b):
    return jnp.dot(a, b, preferred_element_type=F32)


def dot_nt(a, b):
    return lax.dot_general(a, b, (((1,), (1,)), ((), ())), preferred_element_type=F32)


def place():
    head_at, shard = lax.axis_index("head"), lax.axis_index("tm")
    return head_at & 1, head_at >> 1, shard & 3, shard >> 2


def lane_iota(shape):
    return lax.broadcasted_iota(jnp.int32, shape, 1)


def gelu_mix(x32, term):
    return (x32 + jax.nn.gelu(term, approximate=True)).astype(BF16)


def bands_of(w_ref, j):
    groups, width, _ = w_ref.shape
    bands = []
    for g in range(groups):
        parts = [w_ref[g, :, j * width : (j + 1) * width].astype(F32)]
        if g > 0:
            parts.insert(0, jnp.zeros((width, g * width), F32))
        if g < groups - 1:
            parts.append(jnp.zeros((width, (groups - 1 - g) * width), F32))
        bands.append(jnp.concatenate(parts, axis=1))
    return jnp.concatenate(bands, axis=0).astype(BF16)


def gain_rows(g_ref):
    pieces = g_ref[...].astype(F32)
    gain = jnp.concatenate([pieces[i : i + 1] for i in range(pieces.shape[0])], axis=1)
    return jnp.broadcast_to(gain, (GAIN_ROWS, gain.shape[1])).astype(BF16)


def early_kernel(x_hbm, w_hbm, b_hbm, g_hbm, early_ref, edge_ref, x_ref, w_ref, b_ref, g_ref, sems):
    half = early_ref.shape[0] - GAIN_ROWS
    pairs = (
        (x_hbm.at[half - 2 * RIM :], x_ref), (w_hbm, w_ref), (b_hbm, b_ref), (g_hbm, g_ref)
    )
    copies = [pltpu.make_async_copy(src, dst, sems.at[i]) for i, (src, dst) in enumerate(pairs)]
    for copy in copies:
        copy.start()
    for copy in copies:
        copy.wait()
    edge_ref[...] = x_ref[half + RIM :]
    ext = x_ref[...].astype(F32)
    acc = jnp.zeros((half, ext.shape[1]), F32) + b_ref[...]
    for j in range(KERNEL):
        start = RIM + j * DILATION
        acc += dot_nt(ext[start : start + half].astype(BF16), bands_of(w_ref, j))
    early_ref[0:half] = gelu_mix(ext[2 * RIM :], acc)
    early_ref[half:] = gain_rows(g_ref)


def late_kernel(x_ref, w_ref, b_ref, g_ref, late_ref, band_ref, base_ref):
    half = late_ref.shape[0] - GAIN_ROWS
    x32 = x_ref[0:half].astype(F32)
    ext = jnp.concatenate([jnp.zeros((RIM, x32.shape[1]), F32), x32], axis=0)
    acc = jnp.zeros(x32.shape, F32) + b_ref[...]
    for j in range(KERNEL):
        band = bands_of(w_ref, j)
        if j < KERNEL - 1:
            band_ref[j] = band
        acc += dot_nt(ext[j * DILATION : j * DILATION + half].astype(BF16), band)
    base_ref[0:RIM] = acc[0:RIM]
    base_ref[RIM:] = x32[0:RIM]
    late_ref[0:half] = gelu_mix(x32, acc)
    late_ref[half:] = gain_rows(g_ref)


def fix_kernel(halo_ref, base_ref, band_ref, late_ref, o_ref):
    halo = halo_ref[...].astype(F32)
    ext = jnp.concatenate([halo, jnp.zeros_like(halo)], axis=0)
    acc = base_ref[0:RIM]
    for j in range(KERNEL - 1):
        acc += dot_nt(ext[j * DILATION : j * DILATION + RIM].astype(BF16), band_ref[j])
    o_ref[...] = late_ref[...]
    o_ref[0:RIM] = gelu_mix(base_ref[RIM:], acc)


def qkv_kernel(a_ref, b_ref, y_ref, z_ref, wq, wk, wv, *rest):
    pos_ref = place()
    outs, pack = rest[:-1], rest[-1]
    half = a_ref.shape[0] - GAIN_ROWS
    cols = a_ref.shape[1]
    heads = cols // HEAD_DIM
    core, ychip, low = pos_ref[0], pos_ref[1], pos_ref[2]
    parts = [
        (a_ref, 2 * ychip + core),
        (b_ref, 2 * ychip + 1 - core),
        (y_ref, 2 * (1 - ychip) + core),
        (z_ref, 2 * (1 - ychip) + 1 - core),
    ]
    square = jnp.zeros((half, cols), F32)
    for ref, _ in parts:
        x = ref[0:half].astype(F32)
        square += x * x
    rstd = lax.rsqrt(jnp.sum(square, axis=1, keepdims=True) / (4 * cols) + 1e-06)
    normed = []
    for ref, group in parts:
        gain = ref[half : half + 1].astype(F32)
        normed.append(((ref[0:half].astype(F32) * rstd * gain).astype(BF16), group))

    def project(w):
        total = None
        for x, group in normed:
            term = dot32(x, w[pl.ds(pl.multiple_of(group * cols, cols), cols), :])
            total = term if total is None else total + term
        return total.astype(BF16)

    q, k, v = project(wq), project(wk), project(wv)
    q = (q.astype(F32) * (1.0 / HEAD_DIM**0.5)).astype(BF16)
    for j in range(heads):
        lanes = slice(j * HEAD_DIM, (j + 1) * HEAD_DIM)
        slot = jnp.bitwise_xor(low, j)
        pack[slot, 0:half, :] = jnp.concatenate([k[:, lanes], v[:, lanes]], axis=1)
        pack[slot, half : half + half // 2, :] = jnp.concatenate(
            [q[: half // 2, lanes], q[half // 2 :, lanes]], axis=1
        )
    for m, out in enumerate(outs):
        out[...] = pack[m]


def pack_kernel(*refs):
    kv_ref = refs[-1]
    for i, ref in enumerate(refs[:-1]):
        kv_ref[i] = ref[0 : kv_ref.shape[1], :]


def halves():
    lane = lane_iota((1, 128))
    left = jnp.where(lane < HEAD_DIM, 1.0, 0.0)
    return left.astype(BF16), (1.0 - left).astype(BF16)


def shard_of(pos, side, i):
    return 4 * jnp.bitwise_xor(side, 1 - i // 4) + jnp.bitwise_xor(pos[2], i % 4)


def key_bias(valid_ref, shard, i, half):
    lane = lane_iota((half, 128))
    row = jnp.where(lane == HEAD_DIM, lax.broadcasted_iota(jnp.int32, (half, 128), 0), -1)
    start = (2 * shard + 1 - i // 4) * half
    stretch = start // STRETCH
    first_bad = jnp.maximum(valid_ref[stretch] - (start - stretch * STRETCH), 0)
    return jnp.where(row >= first_bad, NEG, 0.0).astype(BF16)


def own_kernel(valid_ref, kv_ref, *rest):
    pos_ref = place()
    own_refs, (kb, vb, qs_ref, bias_ref) = rest[:8], rest[8:]
    left, right = halves()
    half = kb.shape[1]
    lane = lane_iota((half // 2, 128))
    pad = jnp.where(lane == HEAD_DIM, 1.0, 0.0)
    for i, ref in enumerate(own_refs):
        shard = shard_of(pos_ref, pos_ref[0], i)
        kb[shard] = kv_ref[i] * left + key_bias(valid_ref, shard, i, half)
        vb[shard] = kv_ref[i] * right + left
        bias_ref[i] = key_bias(valid_ref, shard_of(pos_ref, 1 - pos_ref[0], i), i, half)
        packed = ref[half:, :].astype(F32)
        rolled = pltpu.roll(packed, HEAD_DIM, 1)
        qs_ref[shard, 0 : half // 2] = jnp.where(lane < HEAD_DIM, packed, pad).astype(BF16)
        qs_ref[shard, half // 2 :] = jnp.where(lane < HEAD_DIM, rolled, pad).astype(BF16)


def attend_kernel(oth_ref, bias_ref, k_own, v_own, qs, o_ref, k_oth, v_oth, sc):
    ranks = o_ref.shape[0]
    half = o_ref.shape[1] * 2
    halfrows = half // 2
    pos_ref = place()
    core = pos_ref[0]
    lane_h = lane_iota((halfrows, 128))
    left, right = halves()
    for i in range(8):
        shard = shard_of(pos_ref, 1 - core, i)
        k_oth[shard] = oth_ref[i] * left + bias_ref[i]
        v_oth[shard] = oth_ref[i] * right + left
    causal = lane_iota((half, half)) <= lax.broadcasted_iota(jnp.int32, (half, half), 0)
    blocks = [(k_own, v_own), (k_oth, v_oth)]

    def scores(t):
        ahead = jnp.where(jnp.bitwise_xor(core, t // 4) == 0, NEG, 0.0)
        q = qs[t]
        top = jnp.full((half, 128), NEG, F32)
        for b in range(2 * t + 2):
            s = dot_nt(q, blocks[b % 2][0][b // 2])
            if b == 2 * t:
                s = jnp.where(causal, s, NEG)
            elif b == 2 * t + 1:
                s = s + ahead
            sc[t % 2, b] = s
            for piece in range(half // 128):
                top = jnp.maximum(top, s[:, piece * 128 : (piece + 1) * 128])
        return jnp.max(top, axis=1, keepdims=True)

    def values(t, m):
        acc = jnp.zeros((half, 128), F32)
        for b in range(2 * t + 2):
            acc += dot32(jnp.exp(sc[t % 2, b] - m).astype(BF16), blocks[b % 2][1][b // 2])
        out = acc / pltpu.roll(acc, HEAD_DIM, 1)
        left = pltpu.roll(out[:halfrows], HEAD_DIM, 1)
        o_ref[t] = jnp.where(lane_h < HEAD_DIM, left, out[halfrows:]).astype(BF16)

    tops = [scores(0)]
    for t in range(ranks):
        if t < ranks - 1:
            tops.append(scores(t + 1))
        values(t, tops[t])


def features(core, att_ref):
    heads, quarter, _ = att_ref.shape
    lane = lane_iota((quarter, 128))
    feats = []
    for first in (core, 1 - core):
        tops, bots = [], []
        for j in range(0, heads // 2, 2):
            a = att_ref[first * (heads // 2) + j].astype(F32)
            b = att_ref[first * (heads // 2) + j + 1].astype(F32)
            tops.append(jnp.where(lane < HEAD_DIM, a, pltpu.roll(b, HEAD_DIM, 1)))
            bots.append(jnp.where(lane < HEAD_DIM, pltpu.roll(a, HEAD_DIM, 1), b))
        feats.append(
            jnp.concatenate(
                [jnp.concatenate(tops, axis=1), jnp.concatenate(bots, axis=1)], axis=0
            ).astype(BF16)
        )
    return feats


def partial_out(pos_ref, feats, w0, w1, step, cols):
    group = jnp.bitwise_xor(2 * pos_ref[1] + pos_ref[0], step)
    lanes = pl.ds(pl.multiple_of(group * cols, cols), cols)
    return dot32(feats[0], w0[:, lanes]) + dot32(feats[1], w1[:, lanes])


def far_kernel(att_ref, w0, w1, across_ref, corner_ref):
    pos_ref = place()
    feats = features(pos_ref[0], att_ref)
    for step, ref in ((2, across_ref), (3, corner_ref)):
        ref[...] = partial_out(pos_ref, feats, w0, w1, step, ref.shape[1]).astype(BF16)


def rows_of(pos_ref, half, other):
    mine = jnp.bitwise_xor(jnp.bitwise_xor(pos_ref[0], pos_ref[3]), other)
    return pl.ds(pl.multiple_of(mine * half, half), half)


def near_kernel(att_ref, w0, w1, late_ref, early_ref, base_ref, beside_ref):
    pos_ref = place()
    feats = features(pos_ref[0], att_ref)
    half, cols = beside_ref.shape
    beside_ref[...] = partial_out(pos_ref, feats, w0, w1, 1, cols).astype(BF16)
    base_ref[0:half] = late_ref[0:half].astype(F32)
    base_ref[half:] = early_ref[0:half].astype(F32)
    base_ref[rows_of(pos_ref, half, 0)] += partial_out(pos_ref, feats, w0, w1, 0, cols)


def final_kernel(base_ref, beside_ref, across_ref, corner_ref, o_ref):
    pos_ref = place()
    half = beside_ref.shape[0]
    mine, other = rows_of(pos_ref, half, 0), rows_of(pos_ref, half, 1)
    o_ref[mine] = (base_ref[mine] + across_ref[...].astype(F32)).astype(BF16)
    rest = beside_ref[...].astype(F32) + corner_ref[...].astype(F32)
    o_ref[other] = (base_ref[other] + rest).astype(BF16)


def call(kernel, outs, scalars, args, *, us, vmem=16, scratch=(), space=pltpu.VMEM):
    spaces = [pltpu.SMEM] * scalars + [space] * (len(args) - scalars)
    outs = [jax.ShapeDtypeStruct(*out) for out in outs]
    result = pl.pallas_call(
        kernel,
        out_shape=outs,
        in_specs=[pl.BlockSpec(memory_space=space) for space in spaces],
        out_specs=[pl.BlockSpec(memory_space=pltpu.VMEM)] * len(outs),
        scratch_shapes=scratch,
        compiler_params=pltpu.CompilerParams(vmem_limit_bytes=vmem << 20),
        cost_estimate=pl.CostEstimate(
            flops=int(us * 1e9), bytes_accessed=int(us * 3.6e6), transcendentals=0
        ),
    )(*args)
    return result if len(outs) > 1 else result[0]


def on_device(
    tokens_in, conv_weight, conv_bias, norm_gain, w_query, w_key, w_value, w_out, valid_count
):
    tok, cols = tokens_in.shape
    half = tok // 2
    ranks = lax.axis_size("tm")
    operands = (
        tokens_in, jnp.swapaxes(conv_weight, 1, 2),
        conv_bias.reshape(1, cols), norm_gain.reshape(cols // 128, 128),
    )
    early, edge = call(
        early_kernel,
        [((half + GAIN_ROWS, cols), BF16), ((RIM, cols), BF16)],
        0,
        operands,
        us=1.5,
        vmem=CONV_VMEM,
        scratch=[pltpu.VMEM((half + 2 * RIM, cols), BF16)]
        + [pltpu.VMEM(x.shape, x.dtype) for x in operands[1:]]
        + [pltpu.SemaphoreType.DMA((len(operands),))],
        space=pltpu.HBM,
    )
    halo = from_behind(edge, "tm", 1)
    operands = lax.optimization_barrier((*operands, edge))[:4]
    late, band, base = call(
        late_kernel,
        [
            ((half + GAIN_ROWS, cols), BF16),
            ((KERNEL - 1, cols, cols), BF16),
            ((2 * RIM, cols), F32),
        ],
        0,
        operands,
        us=1.0,
    )

    def project_half(x, after=None):
        across = swap(x, 2)
        if after is not None:
            corner = swap(x, 3)
            x = lax.optimization_barrier((x, after))[0]
        else:
            corner = swap(across, 1)
        beside = swap(x, 1)
        return call(
            qkv_kernel,
            [((half + half // 2, 2 * HEAD_DIM), BF16)] * 4,
            0,
            (x, beside, across, corner, w_query, w_key, w_value),
            us=1.0,
            scratch=[pltpu.VMEM((4, half + half // 2, 2 * HEAD_DIM), BF16)],
        )

    sends = list(project_half(early))
    late = call(
        fix_kernel, [((half + GAIN_ROWS, cols), BF16)], 0, (halo, base, band, late), us=FIX_US
    )
    sends += list(project_half(late, sends[0]))
    own = [spread(value, i % 4, 1 - i // 4) for i, value in enumerate(sends)]
    kv = call(pack_kernel, [((8, half, 128), BF16)], 0, own, us=0.4)
    wo1 = swap(lax.optimization_barrier((w_out, sends[0]))[0], 1)
    kv_oth = swap(kv, 1)
    k_own, v_own, qs, bias = call(
        own_kernel, [((8, half, 128), BF16)] * 4, 1, (valid_count, kv, *own), us=0.8
    )
    attended = call(
        attend_kernel,
        [((8, half // 2, 2 * HEAD_DIM), BF16)],
        0,
        (kv_oth, bias, k_own, v_own, qs),
        us=8.0,
        vmem=24,
        scratch=[
            pltpu.VMEM((8, half, 128), BF16),
            pltpu.VMEM((8, half, 128), BF16),
            pltpu.VMEM((2, 16, half, half), F32),
        ],
    )
    back = lax.all_to_all(attended, "tm", 0, 0)
    across, corner = call(
        far_kernel, [((half, cols), BF16)] * 2, 0, (back, w_out, wo1), us=0.6
    )
    across, corner = swap(across, 2), swap(corner, 3)
    base, beside = call(
        near_kernel,
        [((tok, cols), F32), ((half, cols), BF16)],
        0,
        (back, w_out, wo1, late, early),
        us=1.0,
    )
    args = (base, swap(beside, 1), across, corner)
    return call(final_kernel, [((tok, cols), BF16)], 0, args, us=0.5)


def solution(mesh):
    ranks, heads = mesh.shape["tm"], mesh.shape["head"]

    def body(*args):
        tokens_in, conv_weight, *_ = args
        tok, cols = tokens_in.shape
        fits = heads == 4 and cols == 4 * HEAD_DIM and ranks == 2 * (cols // HEAD_DIM)
        fits = fits and tok == 512 and ranks * tok <= (WINDOW + 1) * STRETCH
        return on_device(*args) if fits else ring_on_device(*args)

    return jax.shard_map(
        body,
        mesh=mesh,
        in_specs=(
            P("tm", "head"),
            P("head", None, None),
            P("head"),
            P("head"),
            P(None, "head"),
            P(None, "head"),
            P(None, "head"),
            P("head", None),
            P(),
        ),
        out_specs=P("tm", "head"),
        check_vma=False,
    )
```

```python
import functools

import jax
import jax.numpy as jnp
from jax import lax
from jax.experimental import pallas as pl
from jax.experimental.pallas import tpu as pltpu
from jax.sharding import PartitionSpec as P

D = 1024
HEAD_DIM = 64
KERNEL = 3
DILATION = 4
STRETCH = 1024
WINDOW = 8
RIM = (KERNEL - 1) * DILATION
GAIN_ROWS = 8
CONV_VMEM = 60
FIX_US = 2.0
NEG = -1e30
F32 = jnp.float32
BF16 = jnp.bfloat16


def from_behind(value, axis, steps):
    count = lax.axis_size(axis)
    first, last = (max(0, -steps), min(count, count - steps))
    return lax.ppermute(value, axis, [(source, source + steps) for source in range(first, last)])


def ring_on_device(
    tokens_in, conv_weight, conv_bias, norm_gain, w_query, w_key, w_value, w_out, valid_count
):
    tok = tokens_in.shape[0]
    local_groups = conv_weight.shape[0]
    width = conv_weight.shape[2]
    rim = (KERNEL - 1) * DILATION
    before = from_behind(tokens_in[tok - rim :], "tm", 1)
    extended = jnp.concatenate([before, tokens_in], axis=0)
    taps = [extended[j * DILATION : j * DILATION + tok] for j in range(KERNEL)]
    stacked = jnp.stack(taps, 1).reshape(tok, KERNEL, local_groups, width)
    stacked = jnp.transpose(stacked, (0, 2, 1, 3)).reshape(tok, local_groups, KERNEL * width)
    conv_term = jnp.einsum("tgi,gio->tgo", stacked, conv_weight, preferred_element_type=jnp.float32)
    conv_term = conv_term.reshape(tok, local_groups * width)
    mixed = (
        tokens_in.astype(jnp.float32) + jax.nn.gelu(conv_term + conv_bias, approximate=True)
    ).astype(jnp.bfloat16)
    mixed32 = mixed.astype(jnp.float32)
    weights_all = jnp.concatenate([w_query, w_key, w_value], axis=1)
    local_cols = w_query.shape[1]
    square_part = jnp.sum(mixed32 * mixed32, axis=1)
    square_tot = lax.psum(square_part, "head")
    rstd = lax.rsqrt(square_tot / D + 1e-06)
    normed = (mixed32 * rstd[:, None] * norm_gain.astype(jnp.float32)).astype(jnp.bfloat16)
    projected = jnp.dot(
        lax.all_gather(normed, "head", axis=1, tiled=True),
        weights_all,
        preferred_element_type=jnp.float32,
    )
    projected = projected.astype(jnp.bfloat16)
    local_heads = local_cols // HEAD_DIM
    query = projected[:, :local_cols].reshape(tok, local_heads, HEAD_DIM)
    keys_own = projected[:, local_cols : 2 * local_cols]
    values_own = projected[:, 2 * local_cols :]
    scale = 1.0 / HEAD_DIM**0.5
    shard = lax.axis_index("tm")
    q_pos = shard * tok + jnp.arange(tok, dtype=jnp.int32)
    stretch_ids = jnp.arange(valid_count.shape[0], dtype=jnp.int32)

    def attend(state, keys_blk, values_blk, source):
        top, total, accum = state
        k_pos = source * tok + jnp.arange(tok, dtype=jnp.int32)
        k_stretch = jnp.where(k_pos >= 0, k_pos // STRETCH, -1)
        counts = jnp.sum(
            jnp.where(k_stretch[:, None] == stretch_ids[None, :], valid_count[None, :], 0), axis=1
        )
        key_ok = (k_pos >= 0) & (k_pos % STRETCH < counts)
        allowed = key_ok[None, :] & (k_pos[None, :] <= q_pos[:, None])
        allowed = allowed & (k_pos[None, :] // STRETCH >= q_pos[:, None] // STRETCH - WINDOW)
        keys3 = keys_blk.reshape(tok, local_heads, HEAD_DIM)
        values3 = values_blk.reshape(tok, local_heads, HEAD_DIM)
        scores = (
            jnp.einsum("qhd,khd->hqk", query, keys3, preferred_element_type=jnp.float32) * scale
        )
        block_top = jnp.max(jnp.where(allowed[None], scores, -1e30), axis=2)
        new_top = jnp.maximum(top, block_top)
        weights = jnp.where(allowed[None], jnp.exp(scores - new_top[:, :, None]), 0.0)
        factor = jnp.exp(top - new_top)
        total = total * factor + jnp.sum(weights, axis=2)
        accum = accum * factor[:, :, None] + jnp.einsum(
            "hqk,khd->hqd",
            weights.astype(jnp.bfloat16),
            values3,
            preferred_element_type=jnp.float32,
        )
        return (new_top, total, accum)

    state = (
        jnp.full((local_heads, tok), -1e30, jnp.float32),
        jnp.zeros((local_heads, tok), jnp.float32),
        jnp.zeros((local_heads, tok, HEAD_DIM), jnp.float32),
    )
    state = attend(state, keys_own, values_own, shard)
    reach = (WINDOW * STRETCH + max(STRETCH - tok, 0) + tok - 1) // tok
    steps_back = min(reach, lax.axis_size("tm") - 1)

    def relay_step(step, carry):
        keys_blk, values_blk, inner = carry
        keys_blk, values_blk = from_behind((keys_blk, values_blk), "tm", 1)
        inner = attend(inner, keys_blk, values_blk, shard - step)
        return (keys_blk, values_blk, inner)

    carried = lax.fori_loop(1, steps_back + 1, relay_step, (keys_own, values_own, state))
    state = carried[2]
    top, total, accum = state
    attended = (accum / total[:, :, None]).astype(jnp.bfloat16)
    attended = jnp.transpose(attended, (1, 0, 2)).reshape(tok, local_cols)
    partial_proj = jnp.dot(attended, w_out, preferred_element_type=jnp.float32)
    proj = lax.psum_scatter(
        partial_proj.astype(jnp.bfloat16), "head", scatter_dimension=1, tiled=True
    ).astype(jnp.float32)
    return (mixed32 + proj).astype(jnp.bfloat16)


def swap(value, bit):
    return lax.ppermute(value, "head", [(i, i ^ bit) for i in range(lax.axis_size("head"))])


def spread(value, m, part):
    pairs = []
    for shard in range(8):
        for head_at in range(4):
            b, low, ychip, core = shard // 4, shard % 4, head_at // 2, head_at % 2
            to = (4 * core + (low ^ m)) * 4 + 2 * ychip + (part ^ b)
            pairs.append((shard * 4 + head_at, to))
    return lax.ppermute(value, ("tm", "head"), pairs)


def dot32(a, b):
    return jnp.dot(a, b, preferred_element_type=F32)


def dot_nt(a, b):
    return lax.dot_general(a, b, (((1,), (1,)), ((), ())), preferred_element_type=F32)


def place():
    head_at, shard = lax.axis_index("head"), lax.axis_index("tm")
    return head_at & 1, head_at >> 1, shard & 3, shard >> 2


def lane_iota(shape):
    return lax.broadcasted_iota(jnp.int32, shape, 1)


def gelu_mix(x32, term):
    return (x32 + jax.nn.gelu(term, approximate=True)).astype(BF16)


def bands_of(w_ref, j):
    groups, width, _ = w_ref.shape
    bands = []
    for g in range(groups):
        parts = [w_ref[g, :, j * width : (j + 1) * width].astype(F32)]
        if g > 0:
            parts.insert(0, jnp.zeros((width, g * width), F32))
        if g < groups - 1:
            parts.append(jnp.zeros((width, (groups - 1 - g) * width), F32))
        bands.append(jnp.concatenate(parts, axis=1))
    return jnp.concatenate(bands, axis=0).astype(BF16)


def gain_rows(g_ref):
    pieces = g_ref[...].astype(F32)
    gain = jnp.concatenate([pieces[i : i + 1] for i in range(pieces.shape[0])], axis=1)
    return jnp.broadcast_to(gain, (GAIN_ROWS, gain.shape[1])).astype(BF16)


def early_kernel(x_hbm, w_hbm, b_hbm, g_hbm, early_ref, edge_ref, x_ref, w_ref, b_ref, g_ref, sems):
    half = early_ref.shape[0] - GAIN_ROWS
    pairs = (
        (x_hbm.at[half - 2 * RIM :], x_ref), (w_hbm, w_ref), (b_hbm, b_ref), (g_hbm, g_ref)
    )
    copies = [pltpu.make_async_copy(src, dst, sems.at[i]) for i, (src, dst) in enumerate(pairs)]
    for copy in copies:
        copy.start()
    copies[1].wait()
    bands = [bands_of(w_ref, j) for j in range(KERNEL)]
    for copy in (copies[0], *copies[2:]):
        copy.wait()
    edge_ref[...] = x_ref[half + RIM :]
    ext = x_ref[...].astype(F32)
    acc = jnp.zeros((half, ext.shape[1]), F32) + b_ref[...]
    for j in range(KERNEL):
        start = RIM + j * DILATION
        acc += dot_nt(ext[start : start + half].astype(BF16), bands[j])
    early_ref[0:half] = gelu_mix(ext[2 * RIM :], acc)
    early_ref[half:] = gain_rows(g_ref)


def late_kernel(x_ref, w_ref, b_ref, g_ref, late_ref, band_ref, base_ref):
    half = late_ref.shape[0] - GAIN_ROWS
    x32 = x_ref[0:half].astype(F32)
    ext = jnp.concatenate([jnp.zeros((RIM, x32.shape[1]), F32), x32], axis=0)
    acc = jnp.zeros(x32.shape, F32) + b_ref[...]
    for j in range(KERNEL):
        band = bands_of(w_ref, j)
        if j < KERNEL - 1:
            band_ref[j] = band
        acc += dot_nt(ext[j * DILATION : j * DILATION + half].astype(BF16), band)
    base_ref[0:RIM] = acc[0:RIM]
    base_ref[RIM:] = x32[0:RIM]
    late_ref[0:half] = gelu_mix(x32, acc)
    late_ref[half:] = gain_rows(g_ref)


def fix_kernel(halo_ref, base_ref, band_ref, late_ref, o_ref):
    halo = halo_ref[...].astype(F32)
    ext = jnp.concatenate([halo, jnp.zeros_like(halo)], axis=0)
    acc = base_ref[0:RIM]
    for j in range(KERNEL - 1):
        acc += dot_nt(ext[j * DILATION : j * DILATION + RIM].astype(BF16), band_ref[j])
    o_ref[...] = late_ref[...]
    o_ref[0:RIM] = gelu_mix(base_ref[RIM:], acc)


def qkv_kernel(a_ref, b_ref, y_ref, z_ref, wq, wk, wv, *rest):
    pos_ref = place()
    outs, pack = rest[:-1], rest[-1]
    half = a_ref.shape[0] - GAIN_ROWS
    cols = a_ref.shape[1]
    heads = cols // HEAD_DIM
    core, ychip, low = pos_ref[0], pos_ref[1], pos_ref[2]
    parts = [
        (a_ref, 2 * ychip + core),
        (b_ref, 2 * ychip + 1 - core),
        (y_ref, 2 * (1 - ychip) + core),
        (z_ref, 2 * (1 - ychip) + 1 - core),
    ]
    square = jnp.zeros((half, cols), F32)
    for ref, _ in parts:
        x = ref[0:half].astype(F32)
        square += x * x
    rstd = lax.rsqrt(jnp.sum(square, axis=1, keepdims=True) / (4 * cols) + 1e-06)
    normed = []
    for ref, group in parts:
        gain = ref[half : half + 1].astype(F32)
        normed.append(((ref[0:half].astype(F32) * rstd * gain).astype(BF16), group))

    def project(w):
        total = None
        for x, group in normed:
            term = dot32(x, w[pl.ds(pl.multiple_of(group * cols, cols), cols), :])
            total = term if total is None else total + term
        return total.astype(BF16)

    q, k, v = project(wq), project(wk), project(wv)
    q = (q.astype(F32) * (1.0 / HEAD_DIM**0.5)).astype(BF16)
    for j in range(heads):
        lanes = slice(j * HEAD_DIM, (j + 1) * HEAD_DIM)
        slot = jnp.bitwise_xor(low, j)
        pack[slot, 0:half, :] = jnp.concatenate([k[:, lanes], v[:, lanes]], axis=1)
        pack[slot, half : half + half // 2, :] = jnp.concatenate(
            [q[: half // 2, lanes], q[half // 2 :, lanes]], axis=1
        )
    for m, out in enumerate(outs):
        out[...] = pack[m]


def pack_kernel(*refs):
    kv_ref = refs[-1]
    for i, ref in enumerate(refs[:-1]):
        kv_ref[i] = ref[0 : kv_ref.shape[1], :]


def halves():
    lane = lane_iota((1, 128))
    left = jnp.where(lane < HEAD_DIM, 1.0, 0.0)
    return left.astype(BF16), (1.0 - left).astype(BF16)


def shard_of(pos, side, i):
    return 4 * jnp.bitwise_xor(side, 1 - i // 4) + jnp.bitwise_xor(pos[2], i % 4)


def key_bias(valid_ref, shard, i, half):
    lane = lane_iota((half, 128))
    row = jnp.where(lane == HEAD_DIM, lax.broadcasted_iota(jnp.int32, (half, 128), 0), -1)
    start = (2 * shard + 1 - i // 4) * half
    stretch = start // STRETCH
    first_bad = jnp.maximum(valid_ref[stretch] - (start - stretch * STRETCH), 0)
    return jnp.where(row >= first_bad, NEG, 0.0).astype(BF16)


def own_kernel(valid_ref, kv_ref, *rest):
    pos_ref = place()
    own_refs, (kb, vb, qs_ref, bias_ref) = rest[:8], rest[8:]
    left, right = halves()
    half = kb.shape[1]
    lane = lane_iota((half // 2, 128))
    pad = jnp.where(lane == HEAD_DIM, 1.0, 0.0)
    for i, ref in enumerate(own_refs):
        shard = shard_of(pos_ref, pos_ref[0], i)
        kb[shard] = kv_ref[i] * left + key_bias(valid_ref, shard, i, half)
        vb[shard] = kv_ref[i] * right + left
        bias_ref[i] = key_bias(valid_ref, shard_of(pos_ref, 1 - pos_ref[0], i), i, half)
        packed = ref[half:, :].astype(F32)
        rolled = pltpu.roll(packed, HEAD_DIM, 1)
        qs_ref[shard, 0 : half // 2] = jnp.where(lane < HEAD_DIM, packed, pad).astype(BF16)
        qs_ref[shard, half // 2 :] = jnp.where(lane < HEAD_DIM, rolled, pad).astype(BF16)


def attend_kernel(oth_ref, bias_ref, k_own, v_own, qs, o_ref, k_oth, v_oth, sc):
    ranks = o_ref.shape[0]
    half = o_ref.shape[1] * 2
    halfrows = half // 2
    pos_ref = place()
    core = pos_ref[0]
    lane_h = lane_iota((halfrows, 128))
    left, right = halves()
    for i in range(8):
        shard = shard_of(pos_ref, 1 - core, i)
        k_oth[shard] = oth_ref[i] * left + bias_ref[i]
        v_oth[shard] = oth_ref[i] * right + left
    causal = lane_iota((half, half)) <= lax.broadcasted_iota(jnp.int32, (half, half), 0)
    blocks = [(k_own, v_own), (k_oth, v_oth)]

    def scores(t):
        ahead = jnp.where(jnp.bitwise_xor(core, t // 4) == 0, NEG, 0.0)
        q = qs[t]
        top = jnp.full((half, 128), NEG, F32)
        for b in range(2 * t + 2):
            s = dot_nt(q, blocks[b % 2][0][b // 2])
            if b == 2 * t:
                s = jnp.where(causal, s, NEG)
            elif b == 2 * t + 1:
                s = s + ahead
            sc[t % 2, b] = s
            for piece in range(half // 128):
                top = jnp.maximum(top, s[:, piece * 128 : (piece + 1) * 128])
        return jnp.max(top, axis=1, keepdims=True)

    def values(t, m):
        acc = jnp.zeros((half, 128), F32)
        for b in range(2 * t + 2):
            acc += dot32(jnp.exp(sc[t % 2, b] - m).astype(BF16), blocks[b % 2][1][b // 2])
        out = acc / pltpu.roll(acc, HEAD_DIM, 1)
        left = pltpu.roll(out[:halfrows], HEAD_DIM, 1)
        o_ref[t] = jnp.where(lane_h < HEAD_DIM, left, out[halfrows:]).astype(BF16)

    tops = [scores(0)]
    for t in range(ranks):
        if t < ranks - 1:
            tops.append(scores(t + 1))
        values(t, tops[t])


def features(core, att_ref):
    heads, quarter, _ = att_ref.shape
    lane = lane_iota((quarter, 128))
    feats = []
    for first in (core, 1 - core):
        tops, bots = [], []
        for j in range(0, heads // 2, 2):
            a = att_ref[first * (heads // 2) + j].astype(F32)
            b = att_ref[first * (heads // 2) + j + 1].astype(F32)
            tops.append(jnp.where(lane < HEAD_DIM, a, pltpu.roll(b, HEAD_DIM, 1)))
            bots.append(jnp.where(lane < HEAD_DIM, pltpu.roll(a, HEAD_DIM, 1), b))
        feats.append(
            jnp.concatenate(
                [jnp.concatenate(tops, axis=1), jnp.concatenate(bots, axis=1)], axis=0
            ).astype(BF16)
        )
    return feats


def partial_out(pos_ref, feats, w0, w1, step, cols):
    group = jnp.bitwise_xor(2 * pos_ref[1] + pos_ref[0], step)
    lanes = pl.ds(pl.multiple_of(group * cols, cols), cols)
    return dot32(feats[0], w0[:, lanes]) + dot32(feats[1], w1[:, lanes])


def far_kernel(att_ref, w0, w1, across_ref, corner_ref):
    pos_ref = place()
    feats = features(pos_ref[0], att_ref)
    for step, ref in ((2, across_ref), (3, corner_ref)):
        ref[...] = partial_out(pos_ref, feats, w0, w1, step, ref.shape[1]).astype(BF16)


def rows_of(pos_ref, half, other):
    mine = jnp.bitwise_xor(jnp.bitwise_xor(pos_ref[0], pos_ref[3]), other)
    return pl.ds(pl.multiple_of(mine * half, half), half)


def near_kernel(att_ref, w0, w1, late_ref, early_ref, base_ref, beside_ref):
    pos_ref = place()
    feats = features(pos_ref[0], att_ref)
    half, cols = beside_ref.shape
    beside_ref[...] = partial_out(pos_ref, feats, w0, w1, 1, cols).astype(BF16)
    base_ref[0:half] = late_ref[0:half].astype(F32)
    base_ref[half:] = early_ref[0:half].astype(F32)
    base_ref[rows_of(pos_ref, half, 0)] += partial_out(pos_ref, feats, w0, w1, 0, cols)


def final_kernel(base_ref, beside_ref, across_ref, corner_ref, o_ref):
    pos_ref = place()
    half = beside_ref.shape[0]
    mine, other = rows_of(pos_ref, half, 0), rows_of(pos_ref, half, 1)
    o_ref[mine] = (base_ref[mine] + across_ref[...].astype(F32)).astype(BF16)
    rest = beside_ref[...].astype(F32) + corner_ref[...].astype(F32)
    o_ref[other] = (base_ref[other] + rest).astype(BF16)


def call(kernel, outs, scalars, args, *, us, vmem=16, scratch=(), space=pltpu.VMEM):
    spaces = [pltpu.SMEM] * scalars + [space] * (len(args) - scalars)
    outs = [jax.ShapeDtypeStruct(*out) for out in outs]
    result = pl.pallas_call(
        kernel,
        out_shape=outs,
        in_specs=[pl.BlockSpec(memory_space=space) for space in spaces],
        out_specs=[pl.BlockSpec(memory_space=pltpu.VMEM)] * len(outs),
        scratch_shapes=scratch,
        compiler_params=pltpu.CompilerParams(vmem_limit_bytes=vmem << 20),
        cost_estimate=pl.CostEstimate(
            flops=int(us * 1e9), bytes_accessed=int(us * 3.6e6), transcendentals=0
        ),
    )(*args)
    return result if len(outs) > 1 else result[0]


def on_device(
    tokens_in, conv_weight, conv_bias, norm_gain, w_query, w_key, w_value, w_out, valid_count
):
    tok, cols = tokens_in.shape
    half = tok // 2
    ranks = lax.axis_size("tm")
    operands = (
        tokens_in, jnp.swapaxes(conv_weight, 1, 2),
        conv_bias.reshape(1, cols), norm_gain.reshape(cols // 128, 128),
    )
    early, edge = call(
        early_kernel,
        [((half + GAIN_ROWS, cols), BF16), ((RIM, cols), BF16)],
        0,
        operands,
        us=1.5,
        vmem=CONV_VMEM,
        scratch=[pltpu.VMEM((half + 2 * RIM, cols), BF16)]
        + [pltpu.VMEM(x.shape, x.dtype) for x in operands[1:]]
        + [pltpu.SemaphoreType.DMA((len(operands),))],
        space=pltpu.HBM,
    )
    halo = from_behind(edge, "tm", 1)
    operands = lax.optimization_barrier((*operands, edge))[:4]
    late, band, base = call(
        late_kernel,
        [
            ((half + GAIN_ROWS, cols), BF16),
            ((KERNEL - 1, cols, cols), BF16),
            ((2 * RIM, cols), F32),
        ],
        0,
        operands,
        us=1.0,
    )

    def project_half(x, after=None):
        across = swap(x, 2)
        if after is not None:
            corner = swap(x, 3)
            x = lax.optimization_barrier((x, after))[0]
        else:
            corner = swap(across, 1)
        beside = swap(x, 1)
        return call(
            qkv_kernel,
            [((half + half // 2, 2 * HEAD_DIM), BF16)] * 4,
            0,
            (x, beside, across, corner, w_query, w_key, w_value),
            us=1.0,
            scratch=[pltpu.VMEM((4, half + half // 2, 2 * HEAD_DIM), BF16)],
        )

    sends = list(project_half(early))
    late = call(
        fix_kernel, [((half + GAIN_ROWS, cols), BF16)], 0, (halo, base, band, late), us=FIX_US
    )
    sends += list(project_half(late, sends[0]))
    own = [spread(value, i % 4, 1 - i // 4) for i, value in enumerate(sends)]
    kv = call(pack_kernel, [((8, half, 128), BF16)], 0, own, us=0.4)
    wo1 = swap(lax.optimization_barrier((w_out, sends[0]))[0], 1)
    kv_oth = swap(kv, 1)
    k_own, v_own, qs, bias = call(
        own_kernel, [((8, half, 128), BF16)] * 4, 1, (valid_count, kv, *own), us=0.8
    )
    attended = call(
        attend_kernel,
        [((8, half // 2, 2 * HEAD_DIM), BF16)],
        0,
        (kv_oth, bias, k_own, v_own, qs),
        us=8.0,
        vmem=24,
        scratch=[
            pltpu.VMEM((8, half, 128), BF16),
            pltpu.VMEM((8, half, 128), BF16),
            pltpu.VMEM((2, 16, half, half), F32),
        ],
    )
    back = lax.all_to_all(attended, "tm", 0, 0)
    across, corner = call(
        far_kernel, [((half, cols), BF16)] * 2, 0, (back, w_out, wo1), us=0.6
    )
    across, corner = swap(across, 2), swap(corner, 3)
    base, beside = call(
        near_kernel,
        [((tok, cols), F32), ((half, cols), BF16)],
        0,
        (back, w_out, wo1, late, early),
        us=1.0,
    )
    args = (base, swap(beside, 1), across, corner)
    return call(final_kernel, [((tok, cols), BF16)], 0, args, us=0.5)


def solution(mesh):
    ranks, heads = mesh.shape["tm"], mesh.shape["head"]

    def body(*args):
        tokens_in, conv_weight, *_ = args
        tok, cols = tokens_in.shape
        fits = heads == 4 and cols == 4 * HEAD_DIM and ranks == 2 * (cols // HEAD_DIM)
        fits = fits and tok == 512 and ranks * tok <= (WINDOW + 1) * STRETCH
        return on_device(*args) if fits else ring_on_device(*args)

    return jax.shard_map(
        body,
        mesh=mesh,
        in_specs=(
            P("tm", "head"),
            P("head", None, None),
            P("head"),
            P("head"),
            P(None, "head"),
            P(None, "head"),
            P(None, "head"),
            P("head", None),
            P(),
        ),
        out_specs=P("tm", "head"),
        check_vma=False,
    )
```
